768 devices in a mesh: row: 4 (over x_lo, core), col: 192 (over z, y, x_hi).
Axes of the slice: x: 4 (x_hi: 2, x_lo: 2; x = x_hi * 2 + x_lo), y: 8, z: 12, core: 2. Of those that a mesh axis runs over, the one named last changes fastest.
Arguments:
- tokens: bfloat16 [512, 6144], P('row', 'col'), may hold values from -6 to 6
- gate_weight: bfloat16 [6144, 24576], P('row', 'col'), may hold values from -0.4375 to 0.4375
- up_weight: bfloat16 [6144, 24576], P('row', 'col'), may hold values from -0.4375 to 0.4375
- block_mask: int32 [48, 192], P(None, 'col'), may hold values from 0 to 1, as said below
- cotangent: bfloat16 [512, 24576], P('row', 'col'), may hold values from -6 to 6
Outputs:
- hidden: bfloat16 [512, 24576], P('row', 'col')
- input_grad: bfloat16 [512, 6144], P('row', 'col')
- gate_grad: float32 [6144, 24576], P('row', 'col')
- up_grad: float32 [6144, 24576], P('row', 'col')
The draws below stay inside these ranges and needn't reach their ends.
Inputs may be any that keep to these rules, and one draw needn't show every extreme that they name: `block_mask`: in every block column, each run of 12 block rows that starts at a multiple of 12 holds exactly 6 ones, the others zero.
All inputs are finite; a program needn't handle non-finite values.
Results may differ from the reference program's by a relative error of at most 0.0085.
Values may be sent and summed in bfloat16 or wider, within the bound.
A program may use at most 32 MiB of HBM per device.

```python
import jax
import jax.numpy as jnp
from jax import lax

BLOCK = 128
D = 6144
FF = 24576
TOK_DEV = 128
TOKENS = 512
SEGB = 12


def draw_block_mask(key, part):
    groups = D // BLOCK // SEGB
    scores = jax.random.randint(key, (groups, FF // BLOCK, SEGB), 0, 1 << 20)
    scores = scores * SEGB + jnp.arange(SEGB, dtype=jnp.int32)
    order = jnp.argsort(scores, axis=-1)
    placing = jnp.argsort(order, axis=-1)
    chosen = (placing < SEGB // 2).astype(jnp.int32)
    return jnp.transpose(chosen, (0, 2, 1)).reshape(D // BLOCK, FF // BLOCK)


def strengthened(array, rng, source, target, parts, factor):
    owner, partner = [(jnp.arange(array.shape[position]) // (array.shape[position] // parts)).reshape([-1 if axis == position else 1 for axis in range(array.ndim)]) for position in (source, target)]
    chosen = jax.random.permutation(rng, parts)[partner]
    strong = (owner == chosen) | (owner == (partner + parts // 2) % parts)
    return jnp.where(strong, factor * array, array)


def steps_of(own_key, dims, split, low, top_value):
    def one(position, shards_of):
        steps = jax.random.uniform(jax.random.fold_in(jax.random.fold_in(own_key, 6), position), (shards_of,), jnp.float32, low / len(split), top_value / len(split))
        return jnp.repeat(jnp.exp(steps), dims[position] // shards_of).reshape((-1,) + (1,) * (len(dims) - position - 1))

    factor_of = one(*split[0])
    for cut in split[1:]:
        factor_of = factor_of * one(*cut)
    return factor_of


def centred(rng, extent, spread, most, split=(), kind=jnp.bfloat16):
    drawn = jax.random.normal(rng, extent, jnp.float32) * spread
    if len(split) > 0:
        drawn = steps_of(rng, extent, split, -0.22, 0.18) * drawn
    return jnp.clip(drawn, min=-most, max=most).astype(kind)


def noise_with(key, extent, spread, reach, pieces, heavy, held_as=jnp.bfloat16):
    entries = spread * jax.random.normal(key, extent, jnp.float32)
    if pieces:
        entries = entries * steps_of(key, extent, pieces, -0.22, 0.18)
    return jnp.clip(strengthened(entries, jax.random.fold_in(key, 3), *heavy), -reach, reach).astype(held_as)


def setup_inputs(seed: int = 0) -> dict:
    keys = jax.random.split(jax.random.key(seed), 6)
    tokens = centred(keys[0], (TOKENS, D), 1.0, 6.0, ((0, 4), (1, 192)))
    gate_weight = noise_with(keys[1], (D, FF), (D // 2) ** -0.5, 0.4375, ((0, 4), (1, 192)), (1, 0, 192, 6.0))
    up_weight = noise_with(keys[2], (D, FF), (D // 2) ** -0.5, 0.4375, ((0, 4), (1, 192)), (1, 0, 192, 6.0))
    block_mask = draw_block_mask(jax.random.fold_in(keys[5], 71), 0)
    cotangent = centred(keys[4], (TOKENS, FF), 1.0, 6.0, ((0, 4), (1, 192)))
    return {"tokens": tokens, "gate_weight": gate_weight, "up_weight": up_weight, "block_mask": block_mask, "cotangent": cotangent}


def reference(tokens, gate_weight, up_weight, block_mask, cotangent):
    expanded = jnp.repeat(jnp.repeat(block_mask, BLOCK, axis=0), BLOCK, axis=1).astype(jnp.bfloat16)
    gate_masked = gate_weight * expanded
    up_masked = up_weight * expanded
    gate = jnp.dot(tokens, gate_masked, preferred_element_type=jnp.float32)
    up_values = jnp.dot(tokens, up_masked, preferred_element_type=jnp.float32)
    sig = jax.nn.sigmoid(gate)
    silu_gate = gate * sig
    hidden = (silu_gate * up_values).astype(jnp.bfloat16)
    cot_float = cotangent.astype(jnp.float32)
    grad_gate = (cot_float * up_values * sig * (1.0 + gate * (1.0 - sig))).astype(jnp.bfloat16)
    grad_up = (cot_float * silu_gate).astype(jnp.bfloat16)
    input_grad = (jnp.dot(grad_gate, gate_masked.T, preferred_element_type=jnp.float32)
                  + jnp.dot(grad_up, up_masked.T, preferred_element_type=jnp.float32)).astype(jnp.bfloat16)
    groups = TOKENS // TOK_DEV
    token_groups = tokens.reshape(groups, TOK_DEV, D)
    gate_groups = grad_gate.reshape(groups, TOK_DEV, FF)
    up_groups = grad_up.reshape(groups, TOK_DEV, FF)

    def add_group(running, group_data):
        token_part, gate_slice, up_slice = group_data
        gate_part = lax.dot_general(token_part, gate_slice, (((0,), (0,)), ((), ())), preferred_element_type=jnp.float32).astype(jnp.bfloat16)
        up_part = lax.dot_general(token_part, up_slice, (((0,), (0,)), ((), ())), preferred_element_type=jnp.float32).astype(jnp.bfloat16)
        gate_part = lax.optimization_barrier(gate_part)
        up_part = lax.optimization_barrier(up_part)
        return (running[0] + gate_part.astype(jnp.float32), running[1] + up_part.astype(jnp.float32)), None

    zeros_grad = jnp.zeros((D, FF), jnp.float32)
    totals, unused = lax.scan(add_group, (zeros_grad, zeros_grad), (token_groups, gate_groups, up_groups))
    mask_float = expanded.astype(jnp.float32)
    return hidden, input_grad, totals[0] * mask_float, totals[1] * mask_float
```

```python
import functools

import jax
import jax.numpy as jnp
from jax import lax
from jax.experimental import pallas as pl
from jax.experimental.pallas import tpu as pltpu
from jax.sharding import PartitionSpec as P

MESH = pl.DeviceIdType.MESH
F32 = jnp.float32
BF16 = jnp.bfloat16
BLOCK = 128
NZ, NY, NH, ROWS = 12, 8, 2, 4
ZG = NZ // ROWS
FEATS = 32
TOK = 128
HZ, HY = NZ // 2, NY // 2
ROW_A = NY * FEATS
ROW_B = NZ * FEATS
KH = ZG * NY * FEATS
STEP_A, STEP_B = 0.65, 0.98


def ring_events(half, step, start):
    events = []
    for s in range(half):
        for direction in (0, 1):
            for chunk in (0, 1):
                if s == half - 1 and chunk != direction:
                    continue
                events.append((start + step * (2 * s + chunk), s, direction, chunk))
    return events


def sum_events(half, step, start):
    events = []
    for s in range(half):
        for direction in (0, 1):
            for chunk in (0, 1):
                if s == 0 and chunk != direction:
                    continue
                events.append((start + step * (2 * s + chunk - 1), s, direction, chunk))
    return events


def kernel(
    tok_ref, wg_ref, wu_ref, mask_ref, cot_ref,
    hid_ref, ig_ref, dg_ref, du_ref,
    own, pb, aA, aB, wcA, wcB, wtA, wtB, gsend, grecv, ggb, pA, pB,
    stA, stB, rA, rB, smA, smB, scA, scB, rsA, rsB, fin, fb,
    p0_send, p0_recv, ya_send, ya_recv, zb_send, zb_recv,
    ga_send, ga_recv, gb_send, gb_recv, x_send, x_recv, w_send, w_recv,
    sa_send, sa_recv, sb_send, sb_recv, ca_send, ca_recv, cb_send, cb_recv, f_send, f_recv,
):
    r = lax.axis_index("row")
    col = lax.axis_index("col")
    h = col % NH
    y = (col // NH) % NY
    z = col // (NH * NY)
    s_row = z // ZG
    t_z = ZG * r + z % ZG

    def at(zz, yy, hh):
        return (zz * NY + yy) * NH + hh

    def remote(src, dst, ssem, rsem, row, c):
        return pltpu.make_async_remote_copy(
            src_ref=src, dst_ref=dst, send_sem=ssem, recv_sem=rsem,
            device_id=(row, c), device_id_type=MESH,
        )

    def to_self(hh):
        return jnp.logical_and(s_row == r, h == hh)

    barrier = pltpu.get_barrier_semaphore()

    def greet(row, c):
        pl.semaphore_signal(barrier, inc=1, device_id=(row, c), device_id_type=MESH)

    for hh in range(NH):
        @pl.when(jnp.logical_not(to_self(hh)))
        def _():
            greet(s_row, at(t_z, y, hh))
    for o in range(1, NY):
        greet(r, at(z, (y + o) % NY, h))
    for o in range(1, NZ):
        greet(r, at((z + o) % NZ, y, h))
    for o in range(1, ROWS):
        greet((r + o) % ROWS, col)
    own[...] = tok_ref[...].astype(F32).T.astype(BF16)
    mirrored = jnp.where(s_row == r, NH - 1, NH)
    pl.semaphore_wait(barrier, (NY - 1) + (NZ - 1) + (ROWS - 1) + mirrored)

    def p0_copy(hh):
        return remote(own, pb.at[h], p0_send.at[hh], p0_recv.at[h], s_row, at(t_z, y, hh))

    for hh in range(NH):
        @pl.when(jnp.logical_not(to_self(hh)))
        def _():
            p0_copy(hh).start()

        @pl.when(to_self(hh))
        def _():
            pb[hh] = own[...]

    for zz in range(ZG):
        for yy in range(NY):
            keep = mask_ref[r * (ZG * NY * NH * FEATS // BLOCK) + zz * (NY * NH * FEATS // BLOCK) + yy * NH * FEATS // BLOCK, 0]
            keep = jnp.full((FEATS, BLOCK), keep.astype(F32), F32).astype(BF16)
            src = (zz * NY + yy) * NH * FEATS
            ra = (zz * NY + yy) * FEATS
            rb = (yy * ZG + zz) * FEATS
            wcA[ra:ra + FEATS, 0:128] = wg_ref[src:src + FEATS, :] * keep
            wcA[ra:ra + FEATS, 128:256] = wu_ref[src:src + FEATS, :] * keep
            wcB[rb:rb + FEATS, 0:128] = wg_ref[src + FEATS:src + 2 * FEATS, :] * keep
            wcB[rb:rb + FEATS, 128:256] = wu_ref[src + FEATS:src + 2 * FEATS, :] * keep

    for hh in range(NH):
        @pl.when(jnp.logical_not(to_self(hh)))
        def _():
            remote(own, pb.at[hh], p0_send.at[hh], p0_recv.at[hh], s_row, at(t_z, y, hh)).wait_recv()
    ya = pl.ds(pl.multiple_of(y * FEATS, FEATS), FEATS)
    zb = pl.ds(pl.multiple_of(z * FEATS, FEATS), FEATS)
    aA[z, ya, :] = pb[0]
    aB[y, zb, :] = pb[1]

    def arrived(dst, rsem, row, c):
        remote(dst, dst, p0_send.at[0], rsem, row, c).wait_recv()

    def ya_copy(o):
        return remote(pb.at[0], aA.at[z, ya], ya_send.at[o - 1], ya_recv.at[o - 1], r, at(z, (y + o) % NY, h))

    def zb_copy(o):
        return remote(pb.at[1], aB.at[y, zb], zb_send.at[o - 1], zb_recv.at[o - 1], r, at((z + o) % NZ, y, h))

    for o in (1, 7, 2, 6, 3, 5, 4):
        ya_copy(o).start()
    for o in (1, 11, 2, 10, 3, 9, 4, 8, 5, 7, 6):
        zb_copy(o).start()

    for c in range(0, KH, 256):
        wtA[:, c:c + 256] = wcA[c:c + 256, :].astype(F32).T.astype(BF16)
        wtB[:, c:c + 256] = wcB[c:c + 256, :].astype(F32).T.astype(BF16)

    def ga_copy(s, direction, chunk):
        step = s if direction == 0 else -s
        part = aA.at[(z - step + NZ) % NZ, pl.ds(chunk * (ROW_A // 2), ROW_A // 2)]
        to = (z + 1) % NZ if direction == 0 else (z + NZ - 1) % NZ
        return remote(part, part, ga_send.at[direction, s, chunk], ga_recv.at[direction, s, chunk], r, at(to, y, h))

    def gb_copy(s, direction, chunk):
        step = s if direction == 0 else -s
        part = aB.at[(y - step + NY) % NY, pl.ds(chunk * (ROW_B // 2), ROW_B // 2)]
        to = (y + 1) % NY if direction == 0 else (y + NY - 1) % NY
        return remote(part, part, gb_send.at[direction, s, chunk], gb_recv.at[direction, s, chunk], r, at(z, to, h))

    def wait_ya(o):
        frm = (y + NY - o) % NY
        arrived(aA.at[z, pl.ds(pl.multiple_of(frm * FEATS, FEATS), FEATS)], ya_recv.at[o - 1], r, at(z, frm, h))

    def wait_zb(o):
        frm = (z + NZ - o) % NZ
        arrived(aB.at[y, pl.ds(pl.multiple_of(frm * FEATS, FEATS), FEATS)], zb_recv.at[o - 1], r, at(frm, y, h))

    def wait_ga(s, direction, chunk):
        frm = (z + NZ - 1) % NZ if direction == 0 else (z + 1) % NZ
        step = s + 1 if direction == 0 else -s - 1
        part = aA.at[(z - step + NZ) % NZ, pl.ds(chunk * (ROW_A // 2), ROW_A // 2)]
        arrived(part, ga_recv.at[direction, s, chunk], r, at(frm, y, h))

    def wait_gb(s, direction, chunk):
        frm = (y + NY - 1) % NY if direction == 0 else (y + 1) % NY
        step = s + 1 if direction == 0 else -s - 1
        part = aB.at[(y - step + NY) % NY, pl.ds(chunk * (ROW_B // 2), ROW_B // 2)]
        arrived(part, gb_recv.at[direction, s, chunk], r, at(z, frm, h))

    for o in range(1, NY):
        wait_ya(o)
    order = [(t, 0, s, d, c) for t, s, d, c in ring_events(HZ, STEP_A, 0.0)]
    order += [(t, 1, s, d, c) for t, s, d, c in ring_events(HY, STEP_B, 0.5)]
    order.sort()
    arrived_b = False
    for _, which, s, d, c in order:
        if which == 1 and not arrived_b:
            arrived_b = True
            for o in range(1, NZ):
                wait_zb(o)
        if s > 0:
            (wait_ga if which == 0 else wait_gb)(s - 1, d, c)
        (ga_copy if which == 0 else gb_copy)(s, d, c).start()
    for half, wait in ((HZ, wait_ga), (HY, wait_gb)):
        wait(half - 2, 0, 1)
        wait(half - 2, 1, 0)
        wait(half - 1, 0, 0)
        wait(half - 1, 1, 1)

    def tokens_a(g):
        return aA[g * ZG:(g + 1) * ZG].reshape(KH, TOK)

    def tokens_b(g):
        return aB[:, g * ZG * FEATS:(g + 1) * ZG * FEATS, :].reshape(KH, TOK)

    for g in (0, 2):
        both = jnp.dot(wtA[...], jnp.concatenate([tokens_a(g), tokens_a(g + 1)], axis=1), preferred_element_type=F32)
        both += jnp.dot(wtB[...], jnp.concatenate([tokens_b(g), tokens_b(g + 1)], axis=1), preferred_element_type=F32)
        gsend[g] = both[:, :TOK]
        gsend[g + 1] = both[:, TOK:]

    def x_copy(o):
        g = (r + o) % ROWS
        return remote(gsend.at[g], grecv.at[o - 1], x_send.at[o - 1], x_recv.at[o - 1], g, col)

    for o in (2, 1, 3):
        x_copy(o).start()
    cot = cot_ref[...].astype(F32).T
    for o in range(1, ROWS):
        arrived(grecv.at[o - 1], x_recv.at[o - 1], (r + ROWS - o) % ROWS, col)
    total = gsend[r] + grecv[0] + grecv[1] + grecv[2]
    gate = total[:128]
    up = total[128:]
    sig = 1.0 / (1.0 + jnp.exp(-gate))
    silu = gate * sig
    ggb[r, 0:128, :] = (cot * up * sig * (1.0 + gate * (1.0 - sig))).astype(BF16)
    ggb[r, 128:256, :] = (cot * silu).astype(BF16)

    def w_copy(o):
        return remote(ggb.at[r], ggb.at[r], w_send.at[o - 1], w_recv.at[o - 1], (r + o) % ROWS, col)

    for o in (2, 1, 3):
        w_copy(o).start()
    hid_ref[...] = (silu * up).T.astype(BF16)
    for o in range(1, ROWS):
        frm = (r + ROWS - o) % ROWS
        arrived(ggb.at[frm], w_recv.at[o - 1], frm, col)

    for g in (0, 2):
        rhs = jnp.concatenate([ggb[g], ggb[g + 1]], axis=1)
        ta = jnp.dot(wcA[...], rhs, preferred_element_type=F32)
        tb = jnp.dot(wcB[...], rhs, preferred_element_type=F32)
        for k in range(2):
            lanes = slice(k * TOK, (k + 1) * TOK)
            for zz in range(ZG):
                pA[(g + k) * ZG + zz] = ta[zz * ROW_A:(zz + 1) * ROW_A, lanes]
            for yy in range(NY):
                pB[yy, (g + k) * ZG * FEATS:(g + k + 1) * ZG * FEATS, :] = tb[yy * ZG * FEATS:(yy + 1) * ZG * FEATS, lanes]

    def sum_ring(n, half, place, rows, terms, first, held, ssem, rsem, device):
        size = rows // 2

        def rows_of(chunk):
            return pl.ds(chunk * size, size)

        def copy(s, d, chunk):
            to = (place + 1) % n if d == 0 else (place + n - 1) % n
            src = first.at[d] if s == 0 else held.at[d, s - 1, rows_of(chunk)]
            return remote(src, held.at[d, s, rows_of(chunk)], ssem.at[d, s, chunk], rsem.at[d, s, chunk], r, device(to))

        def send(s, d, chunk):
            t = (place + half - s) % n if d == 0 else (place + n - half + s) % n
            mine = terms[t, rows_of(chunk), :]
            if s == 0:
                first[d] = mine.astype(BF16)
            elif s == 1 and chunk != d:
                held[d, 0, rows_of(chunk), :] = mine.astype(BF16)
            else:
                copy(s - 1, d, chunk).wait_recv()
                held[d, s - 1, rows_of(chunk), :] = (held[d, s - 1, rows_of(chunk), :].astype(F32) + mine).astype(BF16)
            copy(s, d, chunk).start()

        return copy, send

    copy_a, send_a = sum_ring(NZ, HZ, z, ROW_A, pA, stA, rA, sa_send, sa_recv, lambda to: at(to, y, h))
    copy_b, send_b = sum_ring(NY, HY, y, ROW_B, pB, stB, rB, sb_send, sb_recv, lambda to: at(z, to, h))

    def put(row, dw, keep):
        dg_ref[row:row + FEATS, :] = dw[:, :128] * keep
        du_ref[row:row + FEATS, :] = dw[:, 128:] * keep

    def keep_of(zz, yy):
        return mask_ref[r * (ZG * NY * NH * FEATS // BLOCK) + zz * (NY * NH * FEATS // BLOCK) + yy * NH * FEATS // BLOCK, 0].astype(F32)

    contract_tokens = (((1,), (1,)), ((), ()))

    def grads_a(zz):
        lhs = jnp.concatenate([aA[g * ZG + zz] for g in range(ROWS)], axis=1)
        rhs = jnp.concatenate([ggb[g] for g in range(ROWS)], axis=1)
        dw = lax.dot_general(lhs, rhs, contract_tokens, preferred_element_type=F32)
        for yy in range(NY):
            put((zz * NY + yy) * NH * FEATS, dw[yy * FEATS:(yy + 1) * FEATS], keep_of(zz, yy))

    def grads_b(yy):
        lhs = jnp.concatenate([aB[yy, g * ZG * FEATS:(g + 1) * ZG * FEATS, :] for g in range(ROWS)], axis=1)
        rhs = jnp.concatenate([ggb[g] for g in range(ROWS)], axis=1)
        dw = lax.dot_general(lhs, rhs, contract_tokens, preferred_element_type=F32)
        for zz in range(ZG):
            put(((zz * NY + yy) * NH + 1) * FEATS, dw[zz * FEATS:(zz + 1) * FEATS], keep_of(zz, yy))

    pieces = [functools.partial(grads_a, zz) for zz in range(ZG)] + [functools.partial(grads_b, yy) for yy in range(NY)]
    order = [(t, 0, s, d, c) for t, s, d, c in sum_events(HZ, STEP_A, 0.0)]
    order += [(t, 1, s, d, c) for t, s, d, c in sum_events(HY, STEP_B, 0.1)]
    order.sort()
    sent = 0
    for _, which, s, d, c in order:
        (send_a if which == 0 else send_b)(s, d, c)
        sent += 1
        if sent >= 4 and sent % 3 == 1 and pieces:
            pieces.pop(0)()
    while pieces:
        pieces.pop(0)()

    def ca_copy(o):
        to = (y + o) % NY
        src = scA.at[pl.ds(pl.multiple_of(to * FEATS, FEATS), FEATS)]
        return remote(src, rsA.at[o - 1], ca_send.at[o - 1], ca_recv.at[o - 1], r, at(z, to, h))

    def cb_copy(o):
        to = (z + o) % NZ
        src = scB.at[pl.ds(pl.multiple_of(to * FEATS, FEATS), FEATS)]
        return remote(src, rsB.at[o - 1], cb_send.at[o - 1], cb_recv.at[o - 1], r, at(to, y, h))

    def last_sum(half, place, terms, held, sums, rounded, copy, size):
        for c in range(2):
            rows = slice(c * size, (c + 1) * size)
            for d in range(2):
                copy(half - 1, d, c).wait_recv()
            whole = terms[place, rows, :] + held[0, half - 1, rows, :].astype(F32) + held[1, half - 1, rows, :].astype(F32)
            sums[rows, :] = whole
            rounded[rows, :] = whole.astype(BF16)

    last_sum(HZ, z, pA, rA, smA, scA, copy_a, ROW_A // 2)
    for o in (4, 3, 5, 2, 6, 1, 7):
        ca_copy(o).start()
    last_sum(HY, y, pB, rB, smB, scB, copy_b, ROW_B // 2)
    for o in (6, 5, 7, 4, 8, 3, 9, 2, 10, 1, 11):
        cb_copy(o).start()

    def f_copy(hh):
        return remote(fin.at[hh], fb.at[h], f_send.at[hh], f_recv.at[h], s_row, at(t_z, y, hh))

    whole = smA[ya, :]
    for o in range(1, NY):
        ca_copy(o).wait_recv()
        whole += rsA[o - 1].astype(F32)
    fin[0] = whole
    whole = smB[zb, :]
    for o in range(1, NZ):
        cb_copy(o).wait_recv()
        whole += rsB[o - 1].astype(F32)
    fin[1] = whole
    for hh in range(NH):
        @pl.when(jnp.logical_not(to_self(hh)))
        def _():
            f_copy(hh).start()

        @pl.when(to_self(hh))
        def _():
            fb[hh] = fin[hh]

    for o in range(1, NY):
        ya_copy(o).wait_send()
        ca_copy(o).wait_send()
    for o in range(1, NZ):
        zb_copy(o).wait_send()
        cb_copy(o).wait_send()
    for o in range(1, ROWS):
        x_copy(o).wait_send()
        w_copy(o).wait_send()
    for _, s, d, c in ring_events(HZ, 1.0, 0.0):
        ga_copy(s, d, c).wait_send()
    for _, s, d, c in ring_events(HY, 1.0, 0.0):
        gb_copy(s, d, c).wait_send()
    for _, s, d, c in sum_events(HZ, 1.0, 0.0):
        copy_a(s, d, c).wait_send()
    for _, s, d, c in sum_events(HY, 1.0, 0.0):
        copy_b(s, d, c).wait_send()
    for hh in range(NH):
        @pl.when(jnp.logical_not(to_self(hh)))
        def _():
            p0_copy(hh).wait_send()
            f_copy(hh).wait_send()
            remote(fin.at[hh], fb.at[hh], f_send.at[hh], f_recv.at[hh], s_row, at(t_z, y, hh)).wait_recv()
    ig_ref[...] = (fb[0] + fb[1]).T.astype(BF16)


def body(tokens, gate_weight, up_weight, block_mask, cotangent):
    vmem = pl.BlockSpec(memory_space=pltpu.VMEM)
    dma = pltpu.SemaphoreType.DMA
    return pl.pallas_call(
        kernel,
        out_shape=(
            jax.ShapeDtypeStruct(cotangent.shape, BF16),
            jax.ShapeDtypeStruct(tokens.shape, BF16),
            jax.ShapeDtypeStruct(gate_weight.shape, F32),
            jax.ShapeDtypeStruct(up_weight.shape, F32),
        ),
        in_specs=[vmem, vmem, vmem, pl.BlockSpec(memory_space=pltpu.SMEM), vmem],
        out_specs=(vmem,) * 4,
        scratch_shapes=[
            pltpu.VMEM((FEATS, TOK), BF16),
            pltpu.VMEM((NH, FEATS, TOK), BF16),
            pltpu.VMEM((NZ, ROW_A, TOK), BF16),
            pltpu.VMEM((NY, ROW_B, TOK), BF16),
            pltpu.VMEM((KH, 256), BF16),
            pltpu.VMEM((KH, 256), BF16),
            pltpu.VMEM((256, KH), BF16),
            pltpu.VMEM((256, KH), BF16),
            pltpu.VMEM((ROWS, 256, TOK), F32),
            pltpu.VMEM((ROWS - 1, 256, TOK), F32),
            pltpu.VMEM((ROWS, 256, TOK), BF16),
            pltpu.VMEM((NZ, ROW_A, TOK), F32),
            pltpu.VMEM((NY, ROW_B, TOK), F32),
            pltpu.VMEM((2, ROW_A // 2, TOK), BF16),
            pltpu.VMEM((2, ROW_B // 2, TOK), BF16),
            pltpu.VMEM((2, HZ, ROW_A, TOK), BF16),
            pltpu.VMEM((2, HY, ROW_B, TOK), BF16),
            pltpu.VMEM((ROW_A, TOK), F32),
            pltpu.VMEM((ROW_B, TOK), F32),
            pltpu.VMEM((ROW_A, TOK), BF16),
            pltpu.VMEM((ROW_B, TOK), BF16),
            pltpu.VMEM((NY - 1, FEATS, TOK), BF16),
            pltpu.VMEM((NZ - 1, FEATS, TOK), BF16),
            pltpu.VMEM((NH, FEATS, TOK), F32),
            pltpu.VMEM((NH, FEATS, TOK), F32),
            dma((NH,)), dma((NH,)),
            dma((NY - 1,)), dma((NY - 1,)), dma((NZ - 1,)), dma((NZ - 1,)),
            dma((2, HZ, 2)), dma((2, HZ, 2)), dma((2, HY, 2)), dma((2, HY, 2)),
            dma((ROWS - 1,)), dma((ROWS - 1,)), dma((ROWS - 1,)), dma((ROWS - 1,)),
            dma((2, HZ, 2)), dma((2, HZ, 2)), dma((2, HY, 2)), dma((2, HY, 2)),
            dma((NY - 1,)), dma((NY - 1,)), dma((NZ - 1,)), dma((NZ - 1,)),
            dma((NH,)), dma((NH,)),
        ],
        compiler_params=pltpu.CompilerParams(
            collective_id=0, has_side_effects=True, vmem_limit_bytes=40 << 20
        ),
    )(tokens, gate_weight, up_weight, block_mask, cotangent)


def solution(mesh):
    placed = (P("row", "col"), P("row", "col"), P("row", "col"), P(None, "col"), P("row", "col"))
    return jax.shard_map(
        body,
        mesh=mesh,
        in_specs=placed,
        out_specs=(P("row", "col"), P("row", "col"), P("row", "col"), P("row", "col")),
        check_vma=False,
    )
```

```python
import functools

import jax
import jax.numpy as jnp
from jax import lax
from jax.experimental import pallas as pl
from jax.experimental.pallas import tpu as pltpu
from jax.sharding import PartitionSpec as P

MESH = pl.DeviceIdType.MESH
F32 = jnp.float32
BF16 = jnp.bfloat16
BLOCK = 128
NZ, NY, NH, ROWS = 12, 8, 2, 4
ZG = NZ // ROWS
FEATS = 32
TOK = 128
SEGB = ZG * NY * NH * FEATS // BLOCK
HZ, HY = NZ // 2, NY // 2
ROW_A = NY * FEATS
ROW_B = NZ * FEATS
GROUP_B = ZG * FEATS
FAR_Y = (4, 3, 5, 2, 6, 1, 7)
FAR_Z = (6, 5, 7, 4, 8, 3, 9, 2, 10, 1, 11)
STEP_A, STEP_B = 0.65, 0.98


def ring_events(half, step, start):
    events = []
    for s in range(half):
        for direction in (0, 1):
            for chunk in (0, 1):
                if s == half - 1 and chunk != direction:
                    continue
                events.append((start + step * (2 * s + chunk), s, direction, chunk))
    return events


def sum_events(half, step, start):
    events = []
    for s in range(half):
        for direction in (0, 1):
            for chunk in (0, 1):
                if s == 0 and chunk != direction:
                    continue
                events.append((start + step * (2 * s + chunk - 1), s, direction, chunk))
    return events


def kernel(
    own, wg_hbm, wu_hbm, mask_ref, cot_hbm,
    hid_ref, ig_ref, dg_ref, du_ref,
    wg_ref, wu_ref, cot_ref, load_sem, pb, aA, aB, wA, wB, gg, ggT, dA, dB, qA, qB,
    stA, stB, rA, rB, smA, smB, scA, scB, rsA, rsB, fin, fb,
    h_send, h_recv, ya_send, ya_recv, zb_send, zb_recv, ga_send, ga_recv, gb_send, gb_recv,
    w_send, w_recv, d_send, d_recv,
    sa_send, sa_recv, sb_send, sb_recv, ca_send, ca_recv, cb_send, cb_recv,
):
    r = lax.axis_index("row")
    col = lax.axis_index("col")
    h = col % NH
    y = (col // NH) % NY
    z = col // (NH * NY)
    sibling = r + 1 - 2 * (r % 2)
    across = (r + 2) % ROWS
    diagonal = (sibling + 2) % ROWS

    def at(zz, yy, hh):
        return (zz * NY + yy) * NH + hh

    def remote(src, dst, ssem, rsem, row, c):
        return pltpu.make_async_remote_copy(
            src_ref=src, dst_ref=dst, send_sem=ssem, recv_sem=rsem,
            device_id=(row, c), device_id_type=MESH,
        )

    sent = []

    def go(copy):
        copy.start()
        sent.append(copy)

    def arrived(dst, rsem, row, c):
        remote(dst, dst, h_send.at[0], rsem, row, c).wait_recv()

    loads = [
        pltpu.make_async_copy(src, dst, load_sem.at[i])
        for i, (src, dst) in enumerate(((wg_hbm, wg_ref), (wu_hbm, wu_ref), (cot_hbm, cot_ref)))
    ]

    barrier = pltpu.get_barrier_semaphore()

    def greet(row, c):
        pl.semaphore_signal(barrier, inc=1, device_id=(row, c), device_id_type=MESH)

    for o in FAR_Z:
        greet(r, at((z + o) % NZ, y, h))
    for o in FAR_Y:
        greet(r, at(z, (y + o) % NY, h))
    partner = at(z, y, 1 - h)
    greet(r, partner)
    greet(across, col)
    greet(sibling, col)
    for load in loads:
        load.start()
    pl.semaphore_wait(barrier, (NY - 1) + (NZ - 1) + 3)

    go(remote(own, pb.at[h], h_send.at[0], h_recv.at[0], r, partner))
    pb[h] = own[...]

    def keep_of(zz, yy):
        return mask_ref[0, r * SEGB + zz * (SEGB // ZG) + yy * NH * FEATS // BLOCK].astype(F32)

    loads[0].wait()
    loads[1].wait()
    for zz in range(ZG):
        for yy in range(NY):
            keep = jnp.full((FEATS, BLOCK), keep_of(zz, yy), F32).astype(BF16)
            src = (zz * NY + yy) * NH * FEATS
            ra = slice(yy * FEATS, (yy + 1) * FEATS)
            rb = pl.ds(pl.multiple_of(r * GROUP_B + zz * FEATS, FEATS), FEATS)
            wA[r * ZG + zz, ra, 0:128] = wg_ref[src:src + FEATS, :] * keep
            wA[r * ZG + zz, ra, 128:256] = wu_ref[src:src + FEATS, :] * keep
            wB[yy, rb, 0:128] = wg_ref[src + FEATS:src + 2 * FEATS, :] * keep
            wB[yy, rb, 128:256] = wu_ref[src + FEATS:src + 2 * FEATS, :] * keep

    def weights_of(row):
        return (
            wA.at[pl.ds(row * ZG, ZG)],
            wB.at[:, pl.ds(pl.multiple_of(row * GROUP_B, FEATS), GROUP_B)],
        )

    def hand(which, owner, row):
        for part in range(2):
            ref = weights_of(owner)[part]
            go(remote(ref, ref, w_send.at[which, part], w_recv.at[which, part], row, col))

    def handed(which, owner, row):
        for part in range(2):
            arrived(weights_of(owner)[part], w_recv.at[which, part], row, col)

    hand(1, r, across)
    hand(0, r, sibling)

    arrived(pb.at[1 - h], h_recv.at[0], r, partner)
    ya = pl.ds(pl.multiple_of(y * FEATS, FEATS), FEATS)
    zb = pl.ds(pl.multiple_of(z * FEATS, FEATS), FEATS)

    def ya_copy(o):
        return remote(pb.at[0], aA.at[z, ya], ya_send.at[o - 1], ya_recv.at[o - 1], r, at(z, (y + o) % NY, h))

    def zb_copy(o):
        return remote(pb.at[1], aB.at[y, zb], zb_send.at[o - 1], zb_recv.at[o - 1], r, at((z + o) % NZ, y, h))

    for o in FAR_Y:
        go(ya_copy(o))
    for o in FAR_Z:
        go(zb_copy(o))
    aA[z, ya, :] = pb[0]
    aB[y, zb, :] = pb[1]

    def ga_copy(s, direction, chunk):
        step = s if direction == 0 else -s
        part = aA.at[(z - step + NZ) % NZ, pl.ds(chunk * (ROW_A // 2), ROW_A // 2)]
        to = (z + 1) % NZ if direction == 0 else (z + NZ - 1) % NZ
        return remote(part, part, ga_send.at[direction, s, chunk], ga_recv.at[direction, s, chunk], r, at(to, y, h))

    def gb_copy(s, direction, chunk):
        step = s if direction == 0 else -s
        part = aB.at[(y - step + NY) % NY, pl.ds(chunk * (ROW_B // 2), ROW_B // 2)]
        to = (y + 1) % NY if direction == 0 else (y + NY - 1) % NY
        return remote(part, part, gb_send.at[direction, s, chunk], gb_recv.at[direction, s, chunk], r, at(z, to, h))

    def wait_ya(o):
        frm = (y + NY - o) % NY
        arrived(aA.at[z, pl.ds(pl.multiple_of(frm * FEATS, FEATS), FEATS)], ya_recv.at[o - 1], r, at(z, frm, h))

    def wait_zb(o):
        frm = (z + NZ - o) % NZ
        arrived(aB.at[y, pl.ds(pl.multiple_of(frm * FEATS, FEATS), FEATS)], zb_recv.at[o - 1], r, at(frm, y, h))

    def wait_ga(s, direction, chunk):
        frm = (z + NZ - 1) % NZ if direction == 0 else (z + 1) % NZ
        step = s + 1 if direction == 0 else -s - 1
        part = aA.at[(z - step + NZ) % NZ, pl.ds(chunk * (ROW_A // 2), ROW_A // 2)]
        arrived(part, ga_recv.at[direction, s, chunk], r, at(frm, y, h))

    def wait_gb(s, direction, chunk):
        frm = (y + NY - 1) % NY if direction == 0 else (y + 1) % NY
        step = s + 1 if direction == 0 else -s - 1
        part = aB.at[(y - step + NY) % NY, pl.ds(chunk * (ROW_B // 2), ROW_B // 2)]
        arrived(part, gb_recv.at[direction, s, chunk], r, at(z, frm, h))

    for o in range(1, NY):
        wait_ya(o)
    order = [(t, 0, s, d, c) for t, s, d, c in ring_events(HZ, STEP_A, 0.0)]
    order += [(t, 1, s, d, c) for t, s, d, c in ring_events(HY, STEP_B, 0.5)]
    order.sort()
    arrived_b = False
    for _, which, s, d, c in order:
        if which == 1 and not arrived_b:
            arrived_b = True
            for o in range(1, NZ):
                wait_zb(o)
        if s > 0:
            (wait_ga if which == 0 else wait_gb)(s - 1, d, c)
        go((ga_copy if which == 0 else gb_copy)(s, d, c))
    handed(1, across, across)
    hand(2, across, sibling)
    for half, wait in ((HZ, wait_ga), (HY, wait_gb)):
        wait(half - 2, 0, 1)
        wait(half - 2, 1, 0)
        wait(half - 1, 0, 0)
        wait(half - 1, 1, 1)

    handed(0, sibling, sibling)
    handed(2, diagonal, sibling)

    over_features = (((0,), (0,)), ((), ()))
    both = jnp.zeros((TOK, 256), F32)
    for zz in range(NZ):
        both += lax.dot_general(aA[zz], wA[zz], over_features, preferred_element_type=F32)
    for yy in range(NY):
        both += lax.dot_general(aB[yy], wB[yy], over_features, preferred_element_type=F32)
    gate = both[:, :128]
    up = both[:, 128:]
    loads[2].wait()
    cot = cot_ref[...].astype(F32)
    sig = 1.0 / (1.0 + jnp.exp(-gate))
    silu = gate * sig
    grad_gate = cot * up * sig * (1.0 + gate * (1.0 - sig))
    grad_up = cot * silu
    ggT[0:128, :] = grad_gate.T.astype(BF16)
    ggT[128:256, :] = grad_up.T.astype(BF16)
    gg[:, 0:128] = grad_gate.astype(BF16)
    gg[:, 128:256] = grad_up.astype(BF16)
    hid_ref[...] = (silu * up).astype(BF16)

    def sum_ring(n, half, place, rows, weights, first, held, ssem, rsem, device):
        size = rows // 2

        def rows_of(chunk):
            return pl.ds(chunk * size, size)

        def copy(s, d, chunk):
            to = (place + 1) % n if d == 0 else (place + n - 1) % n
            src = first.at[d] if s == 0 else held.at[d, s - 1, rows_of(chunk)]
            return remote(src, held.at[d, s, rows_of(chunk)], ssem.at[d, s, chunk], rsem.at[d, s, chunk], r, device(to))

        def send(s, d, chunk):
            t = (place + half - s) % n if d == 0 else (place + n - half + s) % n
            mine = jnp.dot(weights[t, rows_of(chunk), :], ggT[...], preferred_element_type=F32)
            if s == 0:
                first[d] = mine.astype(BF16)
            elif s == 1 and chunk != d:
                held[d, 0, rows_of(chunk), :] = mine.astype(BF16)
            else:
                copy(s - 1, d, chunk).wait_recv()
                held[d, s - 1, rows_of(chunk), :] = (held[d, s - 1, rows_of(chunk), :].astype(F32) + mine).astype(BF16)
            go(copy(s, d, chunk))

        return copy, send

    copy_a, send_a = sum_ring(NZ, HZ, z, ROW_A, wA, stA, rA, sa_send, sa_recv, lambda to: at(to, y, h))
    copy_b, send_b = sum_ring(NY, HY, y, ROW_B, wB, stB, rB, sb_send, sb_recv, lambda to: at(z, to, h))

    owners = (r, sibling, across, diagonal)

    def grads_a(i):
        for zz in range(ZG):
            dA[i, zz] = jnp.dot(aA[owners[i] * ZG + zz], gg[...], preferred_element_type=F32).astype(BF16)

    def grads_b(i, some):
        rows = pl.ds(pl.multiple_of(owners[i] * GROUP_B, FEATS), GROUP_B)
        for yy in some:
            dB[i, yy] = jnp.dot(aB[yy, rows, :], gg[...], preferred_element_type=F32).astype(BF16)

    def pass_on(i, slot, part, row):
        src, dst = ((dA, qA), (dB, qB))[part]
        go(remote(src.at[i], dst.at[slot], d_send.at[slot, part], d_recv.at[slot, part], row, col))

    def got(slot, part, row):
        dst = (qA, qB)[part]
        arrived(dst.at[slot], d_recv.at[slot, part], row, col)

    def add_sibling(part):
        got(1, part, sibling)
        mine, other = ((dA, qA), (dB, qB))[part]
        for k in range(mine.shape[1]):
            mine[2, k] = (mine[2, k].astype(F32) + other[1, k].astype(F32)).astype(BF16)
        pass_on(2, 2, part, across)

    low, high = range(NY // 2), range(NY // 2, NY)
    pieces = []
    for i, slot in ((3, 1), (2, None), (1, 0), (0, None)):
        pieces.append(functools.partial(grads_a, i))
        if slot is not None:
            pieces.append(functools.partial(pass_on, i, slot, 0, sibling))
        pieces += [functools.partial(grads_b, i, low), functools.partial(grads_b, i, high)]
        if slot is not None:
            pieces.append(functools.partial(pass_on, i, slot, 1, sibling))
        if i == 2:
            pieces += [functools.partial(add_sibling, 0), functools.partial(add_sibling, 1)]
    order = [(t, 0, s, d, c) for t, s, d, c in sum_events(HZ, STEP_A, 0.0)]
    order += [(t, 1, s, d, c) for t, s, d, c in sum_events(HY, STEP_B, 0.1)]
    order.sort()
    count = 0
    for _, which, s, d, c in order:
        (send_a if which == 0 else send_b)(s, d, c)
        count += 1
        if count >= 4 and pieces:
            pieces.pop(0)()
    while pieces:
        pieces.pop(0)()

    def ca_copy(o):
        to = (y + o) % NY
        src = scA.at[pl.ds(pl.multiple_of(to * FEATS, FEATS), FEATS)]
        return remote(src, rsA.at[o - 1], ca_send.at[o - 1], ca_recv.at[o - 1], r, at(z, to, h))

    def cb_copy(o):
        to = (z + o) % NZ
        src = scB.at[pl.ds(pl.multiple_of(to * FEATS, FEATS), FEATS)]
        return remote(src, rsB.at[o - 1], cb_send.at[o - 1], cb_recv.at[o - 1], r, at(to, y, h))

    def last_sum(half, place, weights, held, sums, rounded, copy, size):
        for c in range(2):
            rows = slice(c * size, (c + 1) * size)
            whole = jnp.dot(weights[place, rows, :], ggT[...], preferred_element_type=F32)
            for d in range(2):
                copy(half - 1, d, c).wait_recv()
            whole += held[0, half - 1, rows, :].astype(F32) + held[1, half - 1, rows, :].astype(F32)
            sums[rows, :] = whole
            rounded[rows, :] = whole.astype(BF16)

    last_sum(HZ, z, wA, rA, smA, scA, copy_a, ROW_A // 2)
    for o in FAR_Y:
        go(ca_copy(o))
    last_sum(HY, y, wB, rB, smB, scB, copy_b, ROW_B // 2)
    for o in FAR_Z:
        go(cb_copy(o))

    whole = smA[ya, :]
    for o in range(1, NY):
        ca_copy(o).wait_recv()
        whole += rsA[o - 1].astype(F32)
    fin[0] = whole
    whole = smB[zb, :]
    for o in range(1, NZ):
        cb_copy(o).wait_recv()
        whole += rsB[o - 1].astype(F32)
    fin[1] = whole
    go(remote(fin.at[1 - h], fb, h_send.at[1], h_recv.at[1], r, partner))

    def put(row, dw, keep):
        dg_ref[row:row + FEATS, :] = dw[:, :128] * keep
        du_ref[row:row + FEATS, :] = dw[:, 128:] * keep

    got(0, 0, sibling)
    got(2, 0, across)
    for zz in range(ZG):
        for yy in range(NY):
            rows = slice(yy * FEATS, (yy + 1) * FEATS)
            dw = dA[0, zz, rows, :].astype(F32) + qA[0, zz, rows, :].astype(F32) + qA[2, zz, rows, :].astype(F32)
            put((zz * NY + yy) * NH * FEATS, dw, keep_of(zz, yy))
    got(0, 1, sibling)
    got(2, 1, across)
    for yy in range(NY):
        for zz in range(ZG):
            rows = slice(zz * FEATS, (zz + 1) * FEATS)
            dw = dB[0, yy, rows, :].astype(F32) + qB[0, yy, rows, :].astype(F32) + qB[2, yy, rows, :].astype(F32)
            put(((zz * NY + yy) * NH + 1) * FEATS, dw, keep_of(zz, yy))

    arrived(fb, h_recv.at[1], r, partner)
    ig_ref[...] = (fin[h] + fb[...]).astype(BF16)
    for copy in sent:
        copy.wait_send()


def body(tokens, gate_weight, up_weight, block_mask, cotangent):
    vmem = pl.BlockSpec(memory_space=pltpu.VMEM)
    dma = pltpu.SemaphoreType.DMA
    hbm = pl.BlockSpec(memory_space=pltpu.HBM)
    hidden, input_grad, gate_grad, up_grad = pl.pallas_call(
        kernel,
        out_shape=(
            jax.ShapeDtypeStruct(cotangent.shape, BF16),
            jax.ShapeDtypeStruct(tokens.shape[::-1], BF16),
            jax.ShapeDtypeStruct(gate_weight.shape, F32),
            jax.ShapeDtypeStruct(up_weight.shape, F32),
        ),
        in_specs=[vmem, hbm, hbm, pl.BlockSpec(memory_space=pltpu.SMEM), hbm],
        out_specs=(vmem,) * 4,
        scratch_shapes=[
            pltpu.VMEM(gate_weight.shape, BF16),
            pltpu.VMEM(up_weight.shape, BF16),
            pltpu.VMEM(cotangent.shape, BF16),
            dma((3,)),
            pltpu.VMEM((NH, FEATS, TOK), BF16),
            pltpu.VMEM((NZ, ROW_A, TOK), BF16),
            pltpu.VMEM((NY, ROW_B, TOK), BF16),
            pltpu.VMEM((NZ, ROW_A, 256), BF16),
            pltpu.VMEM((NY, ROW_B, 256), BF16),
            pltpu.VMEM((TOK, 256), BF16),
            pltpu.VMEM((256, TOK), BF16),
            pltpu.VMEM((ROWS, ZG, ROW_A, 256), BF16),
            pltpu.VMEM((ROWS, NY, GROUP_B, 256), BF16),
            pltpu.VMEM((3, ZG, ROW_A, 256), BF16),
            pltpu.VMEM((3, NY, GROUP_B, 256), BF16),
            pltpu.VMEM((2, ROW_A // 2, TOK), BF16),
            pltpu.VMEM((2, ROW_B // 2, TOK), BF16),
            pltpu.VMEM((2, HZ, ROW_A, TOK), BF16),
            pltpu.VMEM((2, HY, ROW_B, TOK), BF16),
            pltpu.VMEM((ROW_A, TOK), F32),
            pltpu.VMEM((ROW_B, TOK), F32),
            pltpu.VMEM((ROW_A, TOK), BF16),
            pltpu.VMEM((ROW_B, TOK), BF16),
            pltpu.VMEM((NY - 1, FEATS, TOK), BF16),
            pltpu.VMEM((NZ - 1, FEATS, TOK), BF16),
            pltpu.VMEM((NH, FEATS, TOK), F32),
            pltpu.VMEM((FEATS, TOK), F32),
            dma((2,)), dma((2,)),
            dma((NY - 1,)), dma((NY - 1,)), dma((NZ - 1,)), dma((NZ - 1,)),
            dma((2, HZ, 2)), dma((2, HZ, 2)), dma((2, HY, 2)), dma((2, HY, 2)),
            dma((3, 2)), dma((3, 2)), dma((3, 2)), dma((3, 2)),
            dma((2, HZ, 2)), dma((2, HZ, 2)), dma((2, HY, 2)), dma((2, HY, 2)),
            dma((NY - 1,)), dma((NY - 1,)), dma((NZ - 1,)), dma((NZ - 1,)),
        ],
        compiler_params=pltpu.CompilerParams(
            collective_id=0, has_side_effects=True, vmem_limit_bytes=40 << 20
        ),
    )(tokens.T, gate_weight, up_weight, block_mask.T, cotangent)
    return hidden, input_grad.T, gate_grad, up_grad


def solution(mesh):
    placed = (P("row", "col"), P("row", "col"), P("row", "col"), P(None, "col"), P("row", "col"))
    return jax.shard_map(
        body,
        mesh=mesh,
        in_specs=placed,
        out_specs=(P("row", "col"), P("row", "col"), P("row", "col"), P("row", "col")),
        check_vma=False,
    )
```

```python
import functools

import jax
import jax.numpy as jnp
from jax import lax
from jax.experimental import pallas as pl
from jax.experimental.pallas import tpu as pltpu
from jax.sharding import PartitionSpec as P

MESH = pl.DeviceIdType.MESH
F32 = jnp.float32
BF16 = jnp.bfloat16
BLOCK = 128
NZ, NY, NH, ROWS = 12, 8, 2, 4
ZG = NZ // ROWS
FEATS = 32
TOK = 128
SEGB = ZG * NY * NH * FEATS // BLOCK
QY = NY // 2
ROW_A = NY * FEATS
ROW_B = NZ * FEATS
GROUP_B = ZG * FEATS
FAR_Y = (4, 3, 5, 2, 6, 1, 7)
FAR_Z = (6, 5, 7, 4, 8, 3, 9, 2, 10, 1, 11)


def kernel(
    own, wg_hbm, wu_hbm, mask_ref, cot_hbm,
    hid_ref, ig_ref, dg_ref, du_ref,
    wg_ref, wu_ref, cot_ref, load_sem, pb, aA, aB, wA, wB, gg, ggT, dA, dB, qA, qB,
    s1A, s1B, t1A, t1B, u1A, u1B, v1A, v1B, t2A, t2B, v2A, v2B, t3A, t3B, fin, fb,
    h_send, h_recv, w_send, w_recv, d_send, d_recv,
    a1_send, a1_recv, a2_send, a2_recv, a3_send, a3_recv, b1_send, b1_recv, b2_send, b2_recv, b3_send, b3_recv,
    ra1_send, ra1_recv, ra2_send, ra2_recv, ra3_send, ra3_recv,
    rb1_send, rb1_recv, rb2_send, rb2_recv, rb3_send, rb3_recv,
):
    r = lax.axis_index("row")
    col = lax.axis_index("col")
    h = col % NH
    y = (col // NH) % NY
    z = col // (NH * NY)
    k, m = z // ZG, z % ZG
    j, q = y // QY, y % QY
    sibling = r + 1 - 2 * (r % 2)
    across = (r + 2) % ROWS
    diagonal = (sibling + 2) % ROWS

    def at(zz, yy, hh):
        return (zz * NY + yy) * NH + hh

    def remote(src, dst, ssem, rsem, row, c):
        return pltpu.make_async_remote_copy(
            src_ref=src, dst_ref=dst, send_sem=ssem, recv_sem=rsem,
            device_id=(row, c), device_id_type=MESH,
        )

    sent = []

    def go(copy):
        copy.start()
        sent.append(copy)

    def arrived(dst, rsem, row, c):
        remote(dst, dst, h_send.at[0], rsem, row, c).wait_recv()

    loads = [
        pltpu.make_async_copy(src, dst, load_sem.at[i])
        for i, (src, dst) in enumerate(((wg_hbm, wg_ref), (wu_hbm, wu_ref), (cot_hbm, cot_ref)))
    ]

    barrier = pltpu.get_barrier_semaphore()

    def greet(row, c):
        pl.semaphore_signal(barrier, inc=1, device_id=(row, c), device_id_type=MESH)

    for o in FAR_Z:
        greet(r, at((z + o) % NZ, y, h))
    for o in FAR_Y:
        greet(r, at(z, (y + o) % NY, h))
    partner = at(z, y, 1 - h)
    greet(r, partner)
    greet(across, col)
    greet(sibling, col)
    for load in loads:
        load.start()
    pl.semaphore_wait(barrier, (NY - 1) + (NZ - 1) + 3)

    go(remote(own, pb.at[h], h_send.at[0], h_recv.at[0], r, partner))
    pb[h] = own[...]

    def keep_of(zz, yy):
        return mask_ref[0, r * SEGB + zz * (SEGB // ZG) + yy * NH * FEATS // BLOCK].astype(F32)

    loads[0].wait()
    loads[1].wait()
    for zz in range(ZG):
        for yy in range(NY):
            keep = jnp.full((FEATS, BLOCK), keep_of(zz, yy), F32).astype(BF16)
            src = (zz * NY + yy) * NH * FEATS
            ra = slice(yy * FEATS, (yy + 1) * FEATS)
            rb = pl.ds(pl.multiple_of(r * GROUP_B + zz * FEATS, FEATS), FEATS)
            wA[r, zz, ra, 0:128] = wg_ref[src:src + FEATS, :] * keep
            wA[r, zz, ra, 128:256] = wu_ref[src:src + FEATS, :] * keep
            wB[yy // QY, yy % QY, rb, 0:128] = wg_ref[src + FEATS:src + 2 * FEATS, :] * keep
            wB[yy // QY, yy % QY, rb, 128:256] = wu_ref[src + FEATS:src + 2 * FEATS, :] * keep

    def weights_of(row):
        return (
            wA.at[row],
            wB.at[:, :, pl.ds(pl.multiple_of(row * GROUP_B, FEATS), GROUP_B)],
        )

    def hand(which, owner, row):
        for part in range(2):
            ref = weights_of(owner)[part]
            go(remote(ref, ref, w_send.at[which, part], w_recv.at[which, part], row, col))

    def handed(which, owner, row):
        for part in range(2):
            arrived(weights_of(owner)[part], w_recv.at[which, part], row, col)

    hand(1, r, across)
    hand(0, r, sibling)

    arrived(pb.at[1 - h], h_recv.at[0], r, partner)
    ya = pl.ds(pl.multiple_of(y * FEATS, FEATS), FEATS)
    zb = pl.ds(pl.multiple_of(z * FEATS, FEATS), FEATS)

    def a1_copy(o):
        slot = aA.at[k, m, ya]
        return remote(pb.at[0], slot, a1_send.at[o - 1], a1_recv.at[o - 1], r, at((z + ZG * o) % NZ, y, h))

    def b1_copy():
        return remote(pb.at[1], aB.at[j, q, zb], b1_send.at[0], b1_recv.at[0], r, at(z, (y + QY) % NY, h))

    def a2_copy(o):
        part = aA.at[:, m, ya]
        return remote(part, part, a2_send.at[o - 1], a2_recv.at[o - 1], r, at(z, (y + o) % NY, h))

    def b2_copy(o):
        part = aB.at[:, q, zb]
        return remote(part, part, b2_send.at[o - 1], b2_recv.at[o - 1], r, at((z + o) % NZ, y, h))

    z_next, z_last = (z + 1) % NZ, (z + NZ - 1) % NZ
    y_next, y_last, y_next2, y_last2 = (y + 1) % NY, (y + NY - 1) % NY, (y + 2) % NY, (y + NY - 2) % NY
    m_next, m_last = (m + 1) % ZG, (m + ZG - 1) % ZG
    q_next, q_last, q_far = (q + 1) % QY, (q + QY - 1) % QY, (q + 2) % QY

    def a3_copy(d, i):
        part = aA.at[i, m]
        return remote(part, part, a3_send.at[d, i], a3_recv.at[d, i], r, at((z_next, z_last)[d], y, h))

    def b3_copy(d, i):
        part = aB.at[i, q]
        to = ((y_next, y_last)[d] if d < 2 else (y_next2, y_last2)[i])
        return remote(part, part, b3_send.at[d, i], b3_recv.at[d, i], r, at(z, to, h))

    for o in (2, 1, 3):
        go(a1_copy(o))
    go(b1_copy())
    aA[k, m, ya, :] = pb[0]
    aB[j, q, zb, :] = pb[1]
    arrived(aB.at[1 - j, q, zb], b1_recv.at[0], r, at(z, (y + QY) % NY, h))
    for o in FAR_Z:
        go(b2_copy(o))
    for o in range(1, ROWS):
        frm = (z + NZ - ZG * o) % NZ
        arrived(aA.at[frm // ZG, m, ya], a1_recv.at[o - 1], r, at(frm, y, h))
    for o in FAR_Y:
        go(a2_copy(o))
    for o in FAR_Y[::-1]:
        frm = (y + NY - o) % NY
        rows = pl.ds(pl.multiple_of(frm * FEATS, FEATS), FEATS)
        arrived(aA.at[:, m, rows], a2_recv.at[o - 1], r, at(z, frm, h))
    for i in range(ROWS):
        for d in range(2):
            go(a3_copy(d, i))
    for o in FAR_Z[::-1]:
        frm = (z + NZ - o) % NZ
        rows = pl.ds(pl.multiple_of(frm * FEATS, FEATS), FEATS)
        arrived(aB.at[:, q, rows], b2_recv.at[o - 1], r, at(frm, y, h))
    for d, i in ((2, 0), (2, 1), (0, 0), (1, 0), (0, 1), (1, 1)):
        go(b3_copy(d, i))
    handed(1, across, across)
    hand(2, across, sibling)
    for i in range(ROWS):
        for d in range(2):
            arrived(aA.at[i, (m_last, m_next)[d]], a3_recv.at[d, i], r, at((z_last, z_next)[d], y, h))
    for d, i in ((2, 0), (2, 1), (0, 0), (1, 0), (0, 1), (1, 1)):
        part = aB.at[i, (q_last, q_next, q_far)[d]]
        frm = ((y_last, y_next)[d] if d < 2 else (y_last2, y_next2)[i])
        arrived(part, b3_recv.at[d, i], r, at(z, frm, h))
    handed(0, sibling, sibling)
    handed(2, diagonal, sibling)

    over_features = (((0,), (0,)), ((), ()))
    both = jnp.zeros((TOK, 256), F32)
    for zz in range(NZ):
        at_z = (zz // ZG, zz % ZG)
        both += lax.dot_general(aA[at_z], wA[at_z], over_features, preferred_element_type=F32)
    for yy in range(NY):
        at_y = (yy // QY, yy % QY)
        both += lax.dot_general(aB[at_y], wB[at_y], over_features, preferred_element_type=F32)
    gate = both[:, :128]
    up = both[:, 128:]
    loads[2].wait()
    cot = cot_ref[...].astype(F32)
    sig = 1.0 / (1.0 + jnp.exp(-gate))
    silu = gate * sig
    grad_gate = cot * up * sig * (1.0 + gate * (1.0 - sig))
    grad_up = cot * silu
    ggT[0:128, :] = grad_gate.T.astype(BF16)
    ggT[128:256, :] = grad_up.T.astype(BF16)
    gg[:, 0:128] = grad_gate.astype(BF16)
    gg[:, 128:256] = grad_up.astype(BF16)
    hid_ref[...] = (silu * up).astype(BF16)

    def terms(weights):
        return jnp.dot(weights, ggT[...], preferred_element_type=F32)

    def ra1_copy(d, i):
        return remote(s1A.at[d, i], t1A.at[d, i], ra1_send.at[d, i], ra1_recv.at[d, i], r, at((z_next, z_last)[d], y, h))

    def rb1_copy(d, i):
        to = ((y_next, y_last)[d] if d < 2 else (y_next2, y_last2)[i])
        return remote(s1B.at[d, i], t1B.at[d, i], rb1_send.at[d, i], rb1_recv.at[d, i], r, at(z, to, h))

    def ra2_copy(o):
        to = (y + o) % NY
        src = v1A.at[:, pl.ds(pl.multiple_of(to * FEATS, FEATS), FEATS)]
        return remote(src, t2A.at[o - 1], ra2_send.at[o - 1], ra2_recv.at[o - 1], r, at(z, to, h))

    def rb2_copy(o):
        to = (z + o) % NZ
        src = v1B.at[:, pl.ds(pl.multiple_of(to * FEATS, FEATS), FEATS)]
        return remote(src, t2B.at[o - 1], rb2_send.at[o - 1], rb2_recv.at[o - 1], r, at(to, y, h))

    def ra3_copy(o):
        to = (z + ZG * o) % NZ
        return remote(v2A.at[to // ZG], t3A.at[o - 1], ra3_send.at[o - 1], ra3_recv.at[o - 1], r, at(to, y, h))

    def rb3_copy():
        return remote(v2B.at[1 - j], t3B, rb3_send.at[0], rb3_recv.at[0], r, at(z, (y + QY) % NY, h))

    for i in range(2):
        s1B[2, i] = terms(wB[i, q_far]).astype(BF16)
        go(rb1_copy(2, i))
        for d in range(2):
            s1A[d, i] = terms(wA[i, (m_next, m_last)[d]]).astype(BF16)
            go(ra1_copy(d, i))
    for i in range(2):
        for d in range(2):
            s1B[d, i] = terms(wB[i, (q_next, q_last)[d]]).astype(BF16)
            go(rb1_copy(d, i))
            s1A[d, 2 + i] = terms(wA[2 + i, (m_next, m_last)[d]]).astype(BF16)
            go(ra1_copy(d, 2 + i))

    owners = (r, sibling, across, diagonal)

    def grads_a(i):
        for zz in range(ZG):
            dA[i, zz] = jnp.dot(aA[owners[i], zz], gg[...], preferred_element_type=F32).astype(BF16)

    def grads_b(i, some):
        rows = pl.ds(pl.multiple_of(owners[i] * GROUP_B, FEATS), GROUP_B)
        for yy in some:
            dB[i, yy] = jnp.dot(aB[yy // QY, yy % QY, rows, :], gg[...], preferred_element_type=F32).astype(BF16)

    def pass_on(i, slot, part, row):
        src, dst = ((dA, qA), (dB, qB))[part]
        go(remote(src.at[i], dst.at[slot], d_send.at[slot, part], d_recv.at[slot, part], row, col))

    def got(slot, part, row):
        dst = (qA, qB)[part]
        arrived(dst.at[slot], d_recv.at[slot, part], row, col)

    def add_sibling(part):
        got(1, part, sibling)
        mine, other = ((dA, qA), (dB, qB))[part]
        for i in range(mine.shape[1]):
            mine[2, i] = (mine[2, i].astype(F32) + other[1, i].astype(F32)).astype(BF16)
        pass_on(2, 2, part, across)

    every = range(NY)
    for i, slot in ((3, 1), (2, None)):
        grads_a(i)
        if slot is not None:
            pass_on(i, slot, 0, sibling)
        grads_b(i, every)
        if slot is not None:
            pass_on(i, slot, 1, sibling)
    for i in range(ROWS):
        u1A[i] = terms(wA[i, m])
    for i in range(2):
        u1B[i] = terms(wB[i, q])
    add_sibling(0)
    add_sibling(1)

    for i in range(ROWS):
        for d in range(2):
            ra1_copy(d, i).wait_recv()
        total = u1A[i] + t1A[0, i].astype(F32) + t1A[1, i].astype(F32)
        u1A[i] = total
        v1A[i] = total.astype(BF16)
    for o in FAR_Y:
        go(ra2_copy(o))
    for i in range(2):
        for d in (2, 0, 1):
            rb1_copy(d, i).wait_recv()
        total = u1B[i] + t1B[0, i].astype(F32) + t1B[1, i].astype(F32) + t1B[2, i].astype(F32)
        u1B[i] = total
        v1B[i] = total.astype(BF16)
    for o in FAR_Z:
        go(rb2_copy(o))

    grads_a(1)
    pass_on(1, 0, 0, sibling)
    grads_b(1, every)
    pass_on(1, 0, 1, sibling)

    total = u1A[:, ya, :]
    for o in FAR_Y[::-1]:
        ra2_copy(o).wait_recv()
        total += t2A[o - 1].astype(F32)
    v2A[...] = total.astype(BF16)
    fin[0:ROWS] = total
    for o in (2, 1, 3):
        go(ra3_copy(o))
    total = u1B[:, zb, :]
    for o in FAR_Z[::-1]:
        rb2_copy(o).wait_recv()
        total += t2B[o - 1].astype(F32)
    v2B[...] = total.astype(BF16)
    fin[ROWS:ROWS + 2] = total
    go(rb3_copy())

    grads_a(0)
    grads_b(0, every)

    total = fin[k]
    for o in (1, 3, 2):
        ra3_copy(o).wait_recv()
        total += t3A[o - 1].astype(F32)
    fin[ROWS + 2] = total
    rb3_copy().wait_recv()
    fin[ROWS + 3] = fin[ROWS + j] + t3B[...].astype(F32)
    go(remote(fin.at[ROWS + 3 - h], fb, h_send.at[1], h_recv.at[1], r, partner))

    def put(row, dw, keep):
        dg_ref[row:row + FEATS, :] = dw[:, :128] * keep
        du_ref[row:row + FEATS, :] = dw[:, 128:] * keep

    got(0, 0, sibling)
    got(2, 0, across)
    for zz in range(ZG):
        for yy in range(NY):
            rows = slice(yy * FEATS, (yy + 1) * FEATS)
            dw = dA[0, zz, rows, :].astype(F32) + qA[0, zz, rows, :].astype(F32) + qA[2, zz, rows, :].astype(F32)
            put((zz * NY + yy) * NH * FEATS, dw, keep_of(zz, yy))
    got(0, 1, sibling)
    got(2, 1, across)
    for yy in range(NY):
        for zz in range(ZG):
            rows = slice(zz * FEATS, (zz + 1) * FEATS)
            dw = dB[0, yy, rows, :].astype(F32) + qB[0, yy, rows, :].astype(F32) + qB[2, yy, rows, :].astype(F32)
            put(((zz * NY + yy) * NH + 1) * FEATS, dw, keep_of(zz, yy))

    arrived(fb, h_recv.at[1], r, partner)
    ig_ref[...] = (fin[ROWS + 2 + h] + fb[...]).astype(BF16)
    for copy in sent:
        copy.wait_send()


def body(tokens, gate_weight, up_weight, block_mask, cotangent):
    vmem = pl.BlockSpec(memory_space=pltpu.VMEM)
    dma = pltpu.SemaphoreType.DMA
    hbm = pl.BlockSpec(memory_space=pltpu.HBM)
    hidden, input_grad, gate_grad, up_grad = pl.pallas_call(
        kernel,
        out_shape=(
            jax.ShapeDtypeStruct(cotangent.shape, BF16),
            jax.ShapeDtypeStruct(tokens.shape[::-1], BF16),
            jax.ShapeDtypeStruct(gate_weight.shape, F32),
            jax.ShapeDtypeStruct(up_weight.shape, F32),
        ),
        in_specs=[vmem, hbm, hbm, pl.BlockSpec(memory_space=pltpu.SMEM), hbm],
        out_specs=(vmem,) * 4,
        scratch_shapes=[
            pltpu.VMEM(gate_weight.shape, BF16),
            pltpu.VMEM(up_weight.shape, BF16),
            pltpu.VMEM(cotangent.shape, BF16),
            dma((3,)),
            pltpu.VMEM((NH, FEATS, TOK), BF16),
            pltpu.VMEM((ROWS, ZG, ROW_A, TOK), BF16),
            pltpu.VMEM((2, QY, ROW_B, TOK), BF16),
            pltpu.VMEM((ROWS, ZG, ROW_A, 256), BF16),
            pltpu.VMEM((2, QY, ROW_B, 256), BF16),
            pltpu.VMEM((TOK, 256), BF16),
            pltpu.VMEM((256, TOK), BF16),
            pltpu.VMEM((ROWS, ZG, ROW_A, 256), BF16),
            pltpu.VMEM((ROWS, NY, GROUP_B, 256), BF16),
            pltpu.VMEM((3, ZG, ROW_A, 256), BF16),
            pltpu.VMEM((3, NY, GROUP_B, 256), BF16),
            pltpu.VMEM((2, ROWS, ROW_A, TOK), BF16),
            pltpu.VMEM((3, 2, ROW_B, TOK), BF16),
            pltpu.VMEM((2, ROWS, ROW_A, TOK), BF16),
            pltpu.VMEM((3, 2, ROW_B, TOK), BF16),
            pltpu.VMEM((ROWS, ROW_A, TOK), F32),
            pltpu.VMEM((2, ROW_B, TOK), F32),
            pltpu.VMEM((ROWS, ROW_A, TOK), BF16),
            pltpu.VMEM((2, ROW_B, TOK), BF16),
            pltpu.VMEM((NY - 1, ROWS, FEATS, TOK), BF16),
            pltpu.VMEM((NZ - 1, 2, FEATS, TOK), BF16),
            pltpu.VMEM((ROWS, FEATS, TOK), BF16),
            pltpu.VMEM((2, FEATS, TOK), BF16),
            pltpu.VMEM((ROWS - 1, FEATS, TOK), BF16),
            pltpu.VMEM((FEATS, TOK), BF16),
            pltpu.VMEM((ROWS + 4, FEATS, TOK), F32),
            pltpu.VMEM((FEATS, TOK), F32),
            dma((2,)), dma((2,)), dma((3, 2)), dma((3, 2)), dma((3, 2)), dma((3, 2)),
            *[dma(n) for n in ((ROWS - 1,), (NY - 1,), (2, ROWS), (1,), (NZ - 1,), (3, 2)) for _ in range(2)],
            *[dma(n) for n in ((2, ROWS), (NY - 1,), (ROWS - 1,), (3, 2), (NZ - 1,), (1,)) for _ in range(2)],
        ],
        compiler_params=pltpu.CompilerParams(
            collective_id=0, has_side_effects=True, vmem_limit_bytes=40 << 20
        ),
    )(tokens.T, gate_weight, up_weight, block_mask.T, cotangent)
    return hidden, input_grad.T, gate_grad, up_grad


def solution(mesh):
    placed = (P("row", "col"), P("row", "col"), P("row", "col"), P(None, "col"), P("row", "col"))
    return jax.shard_map(
        body,
        mesh=mesh,
        in_specs=placed,
        out_specs=(P("row", "col"), P("row", "col"), P("row", "col"), P("row", "col")),
        check_vma=False,
    )
```

```python
import functools

import jax
import jax.numpy as jnp
from jax import lax
from jax.experimental import pallas as pl
from jax.experimental.pallas import tpu as pltpu
from jax.sharding import PartitionSpec as P

MESH = pl.DeviceIdType.MESH
F32 = jnp.float32
BF16 = jnp.bfloat16
BLOCK = 128
NZ, NY, NH, ROWS = 12, 8, 2, 4
ZG = NZ // ROWS
FEATS = 32
TOK = 128
SEGB = ZG * NY * NH * FEATS // BLOCK
QY = NY // 2
ROW_A = NY * FEATS
ROW_B = NZ * FEATS
GROUP_B = ZG * FEATS
FAR_Y = (4, 3, 5, 2, 6, 1, 7)
FAR_Z = (6, 5, 7, 4, 8, 3, 9, 2, 10, 1, 11)


def kernel(
    own, wg_hbm, wu_hbm, mask_ref, cot_hbm,
    hid_hbm, ig_ref, dg_hbm, du_hbm,
    hid_ref, dg_ref, du_ref, store_sem, wg_ref, wu_ref, cot_ref, load_sem, aA, aB, wA, wB, gg, ggT, dA, dB, qA, qB,
    s1A, s1B, t1A, t1B, u1A, u1B, v1A, v1B, t2A, t2B, v2A, v2B, t3A, t3B, fin,
    w_send, w_recv, d_send, d_recv,
    a1_send, a1_recv, a2_send, a2_recv, a3_send, a3_recv, b1_send, b1_recv, b2_send, b2_recv, b3_send, b3_recv,
    ra1_send, ra1_recv, ra2_send, ra2_recv, ra3_send, ra3_recv,
    rb1_send, rb1_recv, rb2_send, rb2_recv, rb3_send, rb3_recv,
):
    r = lax.axis_index("row")
    col = lax.axis_index("col")
    h = col % NH
    y = (col // NH) % NY
    z = col // (NH * NY)
    k, m = z // ZG, z % ZG
    j, q = y // QY, y % QY
    sibling = r + 1 - 2 * (r % 2)
    across = (r + 2) % ROWS
    diagonal = (sibling + 2) % ROWS

    def at(zz, yy, hh):
        return (zz * NY + yy) * NH + hh

    def remote(src, dst, ssem, rsem, row, c):
        return pltpu.make_async_remote_copy(
            src_ref=src, dst_ref=dst, send_sem=ssem, recv_sem=rsem,
            device_id=(row, c), device_id_type=MESH,
        )

    sent = []

    def go(copy):
        copy.start()
        sent.append(copy)

    def arrived(dst, rsem, row, c):
        remote(dst, dst, w_send.at[0, 0], rsem, row, c).wait_recv()

    loads = [
        pltpu.make_async_copy(src, dst, load_sem.at[i])
        for i, (src, dst) in enumerate(((wg_hbm, wg_ref), (wu_hbm, wu_ref), (cot_hbm, cot_ref)))
    ]

    barrier = pltpu.get_barrier_semaphore()

    def greet(row, c):
        pl.semaphore_signal(barrier, inc=1, device_id=(row, c), device_id_type=MESH)

    for o in FAR_Z:
        greet(r, at((z + o) % NZ, y, h))
    for o in FAR_Y:
        greet(r, at(z, (y + o) % NY, h))
    for o in (2, 1, 3, 0):
        greet(r, at((z + ZG * o) % NZ, y, 1 - h))
    greet(r, at(z, (y + QY) % NY, 1 - h))
    greet(across, col)
    greet(sibling, col)
    for load in loads:
        load.start()
    pl.semaphore_wait(barrier, (NY - 1) + (NZ - 1) + 7)

    ya = pl.ds(pl.multiple_of(y * FEATS, FEATS), FEATS)
    zb = pl.ds(pl.multiple_of(z * FEATS, FEATS), FEATS)

    def a1_copy(o, hh):
        return remote(own, aA.at[k, m, ya], a1_send.at[o, hh], a1_recv.at[o], r, at((z + ZG * o) % NZ, y, hh))

    def b1_copy(e, hh):
        return remote(own, aB.at[j, q, zb], b1_send.at[e, hh], b1_recv.at[e], r, at(z, (y + QY * e) % NY, hh))

    def first_round(plane):
        if plane:
            return [b1_copy(e, hh) for e, hh in ((1, 0), (1, 1), (0, 0))]
        return [a1_copy(o, hh) for o, hh in ((2, 1), (2, 0), (1, 1), (3, 1), (1, 0), (3, 0), (0, 1))]

    @pl.when(h == 0)
    def _():
        for copy in first_round(0):
            copy.start()
        aA[k, m, ya, :] = own[...]

    @pl.when(h == 1)
    def _():
        for copy in first_round(1):
            copy.start()
        aB[j, q, zb, :] = own[...]

    def keep_of(zz, yy):
        return mask_ref[0, r * SEGB + zz * (SEGB // ZG) + yy * NH * FEATS // BLOCK].astype(F32)

    loads[0].wait()
    loads[1].wait()
    for zz in range(ZG):
        for yy in range(NY):
            keep = jnp.full((FEATS, BLOCK), keep_of(zz, yy), F32).astype(BF16)
            src = (zz * NY + yy) * NH * FEATS
            ra = slice(yy * FEATS, (yy + 1) * FEATS)
            rb = pl.ds(pl.multiple_of(r * GROUP_B + zz * FEATS, FEATS), FEATS)
            wA[r, zz, ra, 0:128] = wg_ref[src:src + FEATS, :] * keep
            wA[r, zz, ra, 128:256] = wu_ref[src:src + FEATS, :] * keep
            wB[yy // QY, yy % QY, rb, 0:128] = wg_ref[src + FEATS:src + 2 * FEATS, :] * keep
            wB[yy // QY, yy % QY, rb, 128:256] = wu_ref[src + FEATS:src + 2 * FEATS, :] * keep

    def weights_of(row):
        return (
            wA.at[row],
            wB.at[:, :, pl.ds(pl.multiple_of(row * GROUP_B, FEATS), GROUP_B)],
        )

    def hand(which, owner, row):
        for part in range(2):
            ref = weights_of(owner)[part]
            go(remote(ref, ref, w_send.at[which, part], w_recv.at[which, part], row, col))

    def handed(which, owner, row):
        for part in range(2):
            arrived(weights_of(owner)[part], w_recv.at[which, part], row, col)

    hand(1, r, across)
    hand(0, r, sibling)

    def a2_copy(o):
        part = aA.at[:, m, ya]
        return remote(part, part, a2_send.at[o - 1], a2_recv.at[o - 1], r, at(z, (y + o) % NY, h))

    def b2_copy(o):
        part = aB.at[:, q, zb]
        return remote(part, part, b2_send.at[o - 1], b2_recv.at[o - 1], r, at((z + o) % NZ, y, h))

    z_next, z_last = (z + 1) % NZ, (z + NZ - 1) % NZ
    y_next, y_last, y_next2, y_last2 = (y + 1) % NY, (y + NY - 1) % NY, (y + 2) % NY, (y + NY - 2) % NY
    m_next, m_last = (m + 1) % ZG, (m + ZG - 1) % ZG
    q_next, q_last, q_far = (q + 1) % QY, (q + QY - 1) % QY, (q + 2) % QY

    def group_a(g):
        return pl.ds(pl.multiple_of((j + g) % 2 * (QY * FEATS), FEATS), QY * FEATS)

    def group_b(g):
        return pl.ds(pl.multiple_of((k + g) % ROWS * GROUP_B, FEATS), GROUP_B)

    y_to = (y_next, y_last, y_next2, y_last2)
    y_from = (y_last, y_next, y_last2, y_next2)

    def a3_copy(d, g):
        part = aA.at[:, m, group_a(g)]
        return remote(part, part, a3_send.at[d, g], a3_recv.at[d, g], r, at((z_next, z_last)[d], y, h))

    def b3_copy(d, g):
        part = aB.at[:, q, group_b(g)] if d < 2 else aB.at[d - 2, q, group_b(g)]
        return remote(part, part, b3_send.at[d, g], b3_recv.at[d, g], r, at(z, y_to[d], h))

    def wait_a2(g):
        for t in range(1 - g, QY):
            frm = (j + g) % 2 * QY + (q + t) % QY
            rows = pl.ds(pl.multiple_of(frm * FEATS, FEATS), FEATS)
            arrived(aA.at[:, m, rows], a2_recv.at[(y + NY - frm) % NY - 1], r, at(z, frm, h))

    def wait_b2(g):
        for t in range(0 if g else 1, ZG):
            frm = (k + g) % ROWS * ZG + (m + t) % ZG
            rows = pl.ds(pl.multiple_of(frm * FEATS, FEATS), FEATS)
            arrived(aB.at[:, q, rows], b2_recv.at[(z + NZ - frm) % NZ - 1], r, at(frm, y, h))

    arrived(aB.at[1 - j, q, zb], b1_recv.at[1], r, at(z, (y + QY) % NY, 1))

    @pl.when(h == 0)
    def _():
        arrived(aB.at[j, q, zb], b1_recv.at[0], r, at(z, y, 1))

    for o in FAR_Z:
        go(b2_copy(o))
    for o in range(1, ROWS):
        frm = (z + NZ - ZG * o) % NZ
        arrived(aA.at[frm // ZG, m, ya], a1_recv.at[o], r, at(frm, y, 0))

    @pl.when(h == 1)
    def _():
        arrived(aA.at[k, m, ya], a1_recv.at[0], r, at(z, y, 0))

    for o in FAR_Y:
        go(a2_copy(o))
    for half, g in ((0, 0), (1, 0), (1, 1), (1, 3), (0, 1), (1, 2)):
        (wait_b2 if half else wait_a2)(g)
        for d in (2, 3, 0, 1) if half else (0, 1):
            go((b3_copy if half else a3_copy)(d, g))
    handed(1, across, across)
    hand(2, across, sibling)
    for half, g in ((0, 0), (1, 0), (1, 1), (1, 3), (0, 1), (1, 2)):
        for d in (2, 3, 0, 1) if half else (0, 1):
            if half:
                cls = (q_last, q_next, q_far, q_far)[d]
                part = aB.at[:, cls, group_b(g)] if d < 2 else aB.at[d - 2, cls, group_b(g)]
                arrived(part, b3_recv.at[d, g], r, at(z, y_from[d], h))
            else:
                arrived(aA.at[:, (m_last, m_next)[d], group_a(g)], a3_recv.at[d, g], r, at((z_last, z_next)[d], y, h))
    handed(0, sibling, sibling)
    handed(2, diagonal, sibling)

    over_features = (((0,), (0,)), ((), ()))
    both = jnp.zeros((TOK, 256), F32)
    for zz in range(NZ):
        at_z = (zz // ZG, zz % ZG)
        both += lax.dot_general(aA[at_z], wA[at_z], over_features, preferred_element_type=F32)
    for yy in range(NY):
        at_y = (yy // QY, yy % QY)
        both += lax.dot_general(aB[at_y], wB[at_y], over_features, preferred_element_type=F32)
    gate = both[:, :128]
    up = both[:, 128:]
    loads[2].wait()
    cot = cot_ref[...].astype(F32)
    sig = 1.0 / (1.0 + jnp.exp(-gate))
    silu = gate * sig
    grad_gate = cot * up * sig * (1.0 + gate * (1.0 - sig))
    grad_up = cot * silu
    ggT[0:128, :] = grad_gate.T.astype(BF16)
    ggT[128:256, :] = grad_up.T.astype(BF16)
    gg[:, 0:128] = grad_gate.astype(BF16)
    gg[:, 128:256] = grad_up.astype(BF16)
    hid_ref[...] = (silu * up).astype(BF16)

    def terms(weights):
        return jnp.dot(weights, ggT[...], preferred_element_type=F32)

    def ra1_copy(d, g):
        rows = group_a(g)
        return remote(
            s1A.at[d, :, rows], t1A.at[d, :, rows], ra1_send.at[d, g], ra1_recv.at[d, g], r, at((z_next, z_last)[d], y, h)
        )

    def rb1_copy(d, g):
        rows = group_b(g)
        src, dst = (s1B.at[d, :, rows], t1B.at[d, :, rows]) if d < 2 else (s1B.at[2, d - 2, rows], t1B.at[2, d - 2, rows])
        return remote(src, dst, rb1_send.at[d, g], rb1_recv.at[d, g], r, at(z, y_to[d], h))

    def ra2_copy(o):
        to = (y + o) % NY
        src = v1A.at[:, pl.ds(pl.multiple_of(to * FEATS, FEATS), FEATS)]
        return remote(src, t2A.at[o - 1], ra2_send.at[o - 1], ra2_recv.at[o - 1], r, at(z, to, h))

    def rb2_copy(o):
        to = (z + o) % NZ
        src = v1B.at[:, pl.ds(pl.multiple_of(to * FEATS, FEATS), FEATS)]
        return remote(src, t2B.at[o - 1], rb2_send.at[o - 1], rb2_recv.at[o - 1], r, at(to, y, h))

    def ra3_copy(o):
        to = (z + ZG * o) % NZ
        return remote(v2A.at[to // ZG], t3A.at[h * ROWS + o], ra3_send.at[o], ra3_recv.at[h * ROWS + o], r, at(to, y, 0))

    def rb3_copy(e):
        to = (y + QY * e) % NY
        return remote(v2B.at[to // QY], t3B.at[2 * h + e], rb3_send.at[e], rb3_recv.at[2 * h + e], r, at(z, to, 1))

    for i in range(2):
        for d in range(3):
            s1B[d, i] = terms(wB[i, (q_next, q_last, q_far)[d]]).astype(BF16)
    for g in (2, 1, 3, 0):
        for d in (2, 3, 0, 1):
            go(rb1_copy(d, g))
    for i in range(ROWS):
        for d in range(2):
            s1A[d, i] = terms(wA[i, (m_next, m_last)[d]]).astype(BF16)
    for g in (1, 0):
        for d in range(2):
            go(ra1_copy(d, g))
    for i in range(2):
        u1B[i] = terms(wB[i, q])
    for i in range(ROWS):
        u1A[i] = terms(wA[i, m])

    owners = (r, sibling, across, diagonal)

    def grads_a(i):
        for zz in range(ZG):
            dA[i, zz] = jnp.dot(aA[owners[i], zz], gg[...], preferred_element_type=F32).astype(BF16)

    def grads_b(i, some):
        rows = pl.ds(pl.multiple_of(owners[i] * GROUP_B, FEATS), GROUP_B)
        for yy in some:
            dB[i, yy] = jnp.dot(aB[yy // QY, yy % QY, rows, :], gg[...], preferred_element_type=F32).astype(BF16)

    def pass_on(i, slot, part, row):
        src, dst = ((dA, qA), (dB, qB))[part]
        go(remote(src.at[i], dst.at[slot], d_send.at[slot, part], d_recv.at[slot, part], row, col))

    def got(slot, part, row):
        dst = (qA, qB)[part]
        arrived(dst.at[slot], d_recv.at[slot, part], row, col)

    def add_sibling(part):
        got(1, part, sibling)
        mine, other = ((dA, qA), (dB, qB))[part]
        for i in range(mine.shape[1]):
            mine[2, i] = (mine[2, i].astype(F32) + other[1, i].astype(F32)).astype(BF16)
        pass_on(2, 2, part, across)

    def add_a(g):
        rows = group_a(g)
        for d in range(2):
            ra1_copy(d, g).wait_recv()
        total = u1A[:, rows, :] + t1A[0, :, rows, :].astype(F32) + t1A[1, :, rows, :].astype(F32)
        u1A[:, rows, :] = total
        v1A[:, rows, :] = total.astype(BF16)
        for t in (2, 1, 3, 0)[:QY - 1 + g]:
            to = (j + g) % 2 * QY + (q + t) % QY
            go(ra2_copy((to + NY - y) % NY))

    def add_b(g):
        rows = group_b(g)
        for d in (2, 3, 0, 1):
            rb1_copy(d, g).wait_recv()
        total = u1B[:, rows, :]
        for d in range(3):
            total += t1B[d, :, rows, :].astype(F32)
        u1B[:, rows, :] = total
        v1B[:, rows, :] = total.astype(BF16)
        for t in (1, 2, 0)[:ZG if g else ZG - 1]:
            to = (k + g) % ROWS * ZG + (m + t) % ZG
            go(rb2_copy((to + NZ - z) % NZ))

    every = range(NY)
    grads_a(3)
    pass_on(3, 1, 0, sibling)
    grads_b(3, every)
    pass_on(3, 1, 1, sibling)
    add_b(2)
    add_a(1)
    grads_a(2)
    grads_b(2, every)
    add_b(1)
    add_sibling(0)
    add_b(3)
    add_sibling(1)
    add_a(0)
    add_b(0)

    grads_a(1)
    pass_on(1, 0, 0, sibling)
    grads_b(1, every)
    pass_on(1, 0, 1, sibling)

    total = u1A[:, ya, :]
    for o in FAR_Y[::-1]:
        ra2_copy(o).wait_recv()
        total += t2A[o - 1].astype(F32)
    v2A[...] = total.astype(BF16)
    fin[0:ROWS] = total
    for o in (2, 1, 3):
        go(ra3_copy(o))

    @pl.when(h == 1)
    def _():
        ra3_copy(0).start()

    total = u1B[:, zb, :]
    for o in FAR_Z[::-1]:
        rb2_copy(o).wait_recv()
        total += t2B[o - 1].astype(F32)
    v2B[...] = total.astype(BF16)
    fin[ROWS:ROWS + 2] = total
    go(rb3_copy(1))

    @pl.when(h == 0)
    def _():
        rb3_copy(0).start()


    grads_a(0)
    grads_b(0, every)

    def put(row, dw, keep):
        dg_ref[row:row + FEATS, :] = dw[:, :128] * keep
        du_ref[row:row + FEATS, :] = dw[:, 128:] * keep

    got(0, 0, sibling)
    got(2, 0, across)
    for zz in range(ZG):
        for yy in range(NY):
            rows = slice(yy * FEATS, (yy + 1) * FEATS)
            dw = dA[0, zz, rows, :].astype(F32) + qA[0, zz, rows, :].astype(F32) + qA[2, zz, rows, :].astype(F32)
            put((zz * NY + yy) * NH * FEATS, dw, keep_of(zz, yy))
    got(0, 1, sibling)
    got(2, 1, across)
    for yy in range(NY):
        for zz in range(ZG):
            rows = slice(zz * FEATS, (zz + 1) * FEATS)
            dw = dB[0, yy, rows, :].astype(F32) + qB[0, yy, rows, :].astype(F32) + qB[2, yy, rows, :].astype(F32)
            put(((zz * NY + yy) * NH + 1) * FEATS, dw, keep_of(zz, yy))

    stores = [
        pltpu.make_async_copy(src, dst, store_sem.at[i])
        for i, (src, dst) in enumerate(((hid_ref, hid_hbm), (dg_ref, dg_hbm), (du_ref, du_hbm)))
    ]
    for store in stores:
        store.start()

    for copy in sent:
        copy.wait_send()

    @pl.when(h == 0)
    def _():
        for copy in first_round(0):
            copy.wait_send()
        rb3_copy(0).wait_send()

    @pl.when(h == 1)
    def _():
        for copy in first_round(1):
            copy.wait_send()
        ra3_copy(0).wait_send()

    @pl.when(h == 0)
    def _():
        total = fin[k]
        for plane, o in ((0, 1), (0, 3), (1, 0), (1, 1), (1, 3), (0, 2), (1, 2)):
            slot = plane * ROWS + o
            arrived(t3A.at[slot], ra3_recv.at[slot], r, at((z + NZ - ZG * o) % NZ, y, plane))
            total += t3A[slot].astype(F32)
        ig_ref[...] = total.astype(BF16)

    @pl.when(h == 1)
    def _():
        total = fin[ROWS + j]
        for plane, e in ((1, 1), (0, 0), (0, 1)):
            slot = 2 * plane + e
            arrived(t3B.at[slot], rb3_recv.at[slot], r, at(z, (y + QY * e) % NY, plane))
            total += t3B[slot].astype(F32)
        ig_ref[...] = total.astype(BF16)

    for store in stores:
        store.wait()


def body(tokens, gate_weight, up_weight, block_mask, cotangent):
    vmem = pl.BlockSpec(memory_space=pltpu.VMEM)
    dma = pltpu.SemaphoreType.DMA
    hbm = pl.BlockSpec(memory_space=pltpu.HBM)
    hidden, input_grad, gate_grad, up_grad = pl.pallas_call(
        kernel,
        out_shape=(
            jax.ShapeDtypeStruct(cotangent.shape, BF16),
            jax.ShapeDtypeStruct(tokens.shape[::-1], BF16),
            jax.ShapeDtypeStruct(gate_weight.shape, F32),
            jax.ShapeDtypeStruct(up_weight.shape, F32),
        ),
        in_specs=[vmem, hbm, hbm, pl.BlockSpec(memory_space=pltpu.SMEM), hbm],
        out_specs=(hbm, vmem, hbm, hbm),
        scratch_shapes=[
            pltpu.VMEM(cotangent.shape, BF16),
            pltpu.VMEM(gate_weight.shape, F32),
            pltpu.VMEM(up_weight.shape, F32),
            dma((3,)),
            pltpu.VMEM(gate_weight.shape, BF16),
            pltpu.VMEM(up_weight.shape, BF16),
            pltpu.VMEM(cotangent.shape, BF16),
            dma((3,)),
            pltpu.VMEM((ROWS, ZG, ROW_A, TOK), BF16),
            pltpu.VMEM((2, QY, ROW_B, TOK), BF16),
            pltpu.VMEM((ROWS, ZG, ROW_A, 256), BF16),
            pltpu.VMEM((2, QY, ROW_B, 256), BF16),
            pltpu.VMEM((TOK, 256), BF16),
            pltpu.VMEM((256, TOK), BF16),
            pltpu.VMEM((ROWS, ZG, ROW_A, 256), BF16),
            pltpu.VMEM((ROWS, NY, GROUP_B, 256), BF16),
            pltpu.VMEM((3, ZG, ROW_A, 256), BF16),
            pltpu.VMEM((3, NY, GROUP_B, 256), BF16),
            pltpu.VMEM((2, ROWS, ROW_A, TOK), BF16),
            pltpu.VMEM((3, 2, ROW_B, TOK), BF16),
            pltpu.VMEM((2, ROWS, ROW_A, TOK), BF16),
            pltpu.VMEM((3, 2, ROW_B, TOK), BF16),
            pltpu.VMEM((ROWS, ROW_A, TOK), F32),
            pltpu.VMEM((2, ROW_B, TOK), F32),
            pltpu.VMEM((ROWS, ROW_A, TOK), BF16),
            pltpu.VMEM((2, ROW_B, TOK), BF16),
            pltpu.VMEM((NY - 1, ROWS, FEATS, TOK), BF16),
            pltpu.VMEM((NZ - 1, 2, FEATS, TOK), BF16),
            pltpu.VMEM((ROWS, FEATS, TOK), BF16),
            pltpu.VMEM((2, FEATS, TOK), BF16),
            pltpu.VMEM((2 * ROWS, FEATS, TOK), BF16),
            pltpu.VMEM((4, FEATS, TOK), BF16),
            pltpu.VMEM((ROWS + 2, FEATS, TOK), F32),
            dma((3, 2)), dma((3, 2)), dma((3, 2)), dma((3, 2)),
            dma((ROWS, NH)), dma((ROWS,)), dma((NY - 1,)), dma((NY - 1,)), dma((2, 2)), dma((2, 2)),
            dma((2, NH)), dma((2,)), dma((NZ - 1,)), dma((NZ - 1,)), dma((4, ROWS)), dma((4, ROWS)),
            dma((2, 2)), dma((2, 2)), dma((NY - 1,)), dma((NY - 1,)), dma((ROWS,)), dma((2 * ROWS,)),
            dma((4, ROWS)), dma((4, ROWS)), dma((NZ - 1,)), dma((NZ - 1,)), dma((2,)), dma((4,)),
        ],
        compiler_params=pltpu.CompilerParams(
            collective_id=0, has_side_effects=True, vmem_limit_bytes=60 << 20
        ),
    )(tokens.T, gate_weight, up_weight, block_mask.T, cotangent)
    return hidden, input_grad.T, gate_grad, up_grad


def solution(mesh):
    placed = (P("row", "col"), P("row", "col"), P("row", "col"), P(None, "col"), P("row", "col"))
    return jax.shard_map(
        body,
        mesh=mesh,
        in_specs=placed,
        out_specs=(P("row", "col"), P("row", "col"), P("row", "col"), P("row", "col")),
        check_vma=False,
    )
```

```python
import functools

import jax
import jax.numpy as jnp
from jax import lax
from jax.experimental import pallas as pl
from jax.experimental.pallas import tpu as pltpu
from jax.sharding import PartitionSpec as P

MESH = pl.DeviceIdType.MESH
F32 = jnp.float32
BF16 = jnp.bfloat16
BLOCK = 128
NZ, NY, NH, ROWS = 12, 8, 2, 4
ZG = NZ // ROWS
FEATS = 32
TOK = 128
SEGB = ZG * NY * NH * FEATS // BLOCK
QY = NY // 2
ROW_A = NY * FEATS
ROW_B = NZ * FEATS
GROUP_B = ZG * FEATS
FAR_Y = (4, 3, 5, 2, 6, 1, 7)
FAR_Z = (6, 5, 7, 4, 8, 3, 9, 2, 10, 1, 11)


def kernel(
    own, wg_hbm, wu_hbm, mask_ref, cot_hbm,
    hid_hbm, ig_ref, dg_hbm, du_hbm,
    hid_ref, dg_ref, du_ref, store_sem, wg_ref, wu_ref, cot_ref, load_sem, aA, aB, wA, wB, gg, ggT, dA, dB, qA, qB,
    s1A, s1B, t1A, t1B, u1A, u1B, v1A, v1B, t2A, t2B, v2A, v2B, t3A, t3B, fin,
    w_send, w_recv, d_send, d_recv,
    a1_send, a1_recv, a2_send, a2_recv, a3_send, a3_recv, b1_send, b1_recv, b2_send, b2_recv, b3_send, b3_recv,
    ra1_send, ra1_recv, ra2_send, ra2_recv, ra3_send, ra3_recv,
    rb1_send, rb1_recv, rb2_send, rb2_recv, rb3_send, rb3_recv,
):
    r = lax.axis_index("row")
    col = lax.axis_index("col")
    h = col % NH
    y = (col // NH) % NY
    z = col // (NH * NY)
    k, m = z // ZG, z % ZG
    j, q = y // QY, y % QY
    sibling = r + 1 - 2 * (r % 2)
    across = (r + 2) % ROWS
    diagonal = (sibling + 2) % ROWS

    def at(zz, yy, hh):
        return (zz * NY + yy) * NH + hh

    def remote(src, dst, ssem, rsem, row, c):
        return pltpu.make_async_remote_copy(
            src_ref=src, dst_ref=dst, send_sem=ssem, recv_sem=rsem,
            device_id=(row, c), device_id_type=MESH,
        )

    sent = []

    def go(copy):
        copy.start()
        sent.append(copy)

    def arrived(dst, rsem, row, c):
        remote(dst, dst, w_send.at[0, 0], rsem, row, c).wait_recv()

    loads = [
        pltpu.make_async_copy(src, dst, load_sem.at[i])
        for i, (src, dst) in enumerate(((wg_hbm, wg_ref), (wu_hbm, wu_ref), (cot_hbm, cot_ref)))
    ]

    barrier = pltpu.get_barrier_semaphore()

    def greet(row, c):
        pl.semaphore_signal(barrier, inc=1, device_id=(row, c), device_id_type=MESH)

    for o in FAR_Z:
        greet(r, at((z + o) % NZ, y, h))
    for o in FAR_Y:
        greet(r, at(z, (y + o) % NY, h))
    for o in (2, 1, 3, 0):
        greet(r, at((z + ZG * o) % NZ, y, 1 - h))
    greet(r, at(z, (y + QY) % NY, 1 - h))
    greet(across, col)
    greet(sibling, col)
    for load in loads:
        load.start()
    pl.semaphore_wait(barrier, (NY - 1) + (NZ - 1) + 7)

    ya = pl.ds(pl.multiple_of(y * FEATS, FEATS), FEATS)
    zb = pl.ds(pl.multiple_of(z * FEATS, FEATS), FEATS)

    def a1_copy(o, hh):
        return remote(own, aA.at[k, m, ya], a1_send.at[o, hh], a1_recv.at[o], r, at((z + ZG * o) % NZ, y, hh))

    def b1_copy(e, hh):
        return remote(own, aB.at[j, q, zb], b1_send.at[e, hh], b1_recv.at[e], r, at(z, (y + QY * e) % NY, hh))

    def first_round(plane):
        if plane:
            return [b1_copy(e, hh) for e, hh in ((1, 0), (1, 1), (0, 0))]
        return [a1_copy(o, hh) for o, hh in ((2, 1), (2, 0), (1, 1), (3, 1), (1, 0), (3, 0), (0, 1))]

    @pl.when(h == 0)
    def _():
        for copy in first_round(0):
            copy.start()
        aA[k, m, ya, :] = own[...]

    @pl.when(h == 1)
    def _():
        for copy in first_round(1):
            copy.start()
        aB[j, q, zb, :] = own[...]

    def keep_of(zz, yy):
        return mask_ref[0, r * SEGB + zz * (SEGB // ZG) + yy * NH * FEATS // BLOCK].astype(F32)

    loads[0].wait()
    loads[1].wait()
    for zz in range(ZG):
        for yy in range(NY):
            keep = jnp.full((FEATS, BLOCK), keep_of(zz, yy), F32).astype(BF16)
            src = (zz * NY + yy) * NH * FEATS
            ra = slice(yy * FEATS, (yy + 1) * FEATS)
            rb = pl.ds(pl.multiple_of(r * GROUP_B + zz * FEATS, FEATS), FEATS)
            wA[r, zz, ra, 0:128] = wg_ref[src:src + FEATS, :] * keep
            wA[r, zz, ra, 128:256] = wu_ref[src:src + FEATS, :] * keep
            wB[yy // QY, yy % QY, rb, 0:128] = wg_ref[src + FEATS:src + 2 * FEATS, :] * keep
            wB[yy // QY, yy % QY, rb, 128:256] = wu_ref[src + FEATS:src + 2 * FEATS, :] * keep

    def weights_of(row):
        return (
            wA.at[row],
            wB.at[:, :, pl.ds(pl.multiple_of(row * GROUP_B, FEATS), GROUP_B)],
        )

    def hand(which, owner, row, parts=(0, 1)):
        for part in parts:
            ref = weights_of(owner)[part]
            go(remote(ref, ref, w_send.at[which, part], w_recv.at[which, part], row, col))

    def handed(which, owner, row, parts=(0, 1)):
        for part in parts:
            arrived(weights_of(owner)[part], w_recv.at[which, part], row, col)

    hand(1, r, across)
    hand(0, r, sibling)

    def a2_copy(o):
        part = aA.at[:, m, ya]
        return remote(part, part, a2_send.at[o - 1], a2_recv.at[o - 1], r, at(z, (y + o) % NY, h))

    def b2_copy(o):
        part = aB.at[:, q, zb]
        return remote(part, part, b2_send.at[o - 1], b2_recv.at[o - 1], r, at((z + o) % NZ, y, h))

    z_next, z_last = (z + 1) % NZ, (z + NZ - 1) % NZ
    y_next, y_last, y_next2, y_last2 = (y + 1) % NY, (y + NY - 1) % NY, (y + 2) % NY, (y + NY - 2) % NY
    m_next, m_last = (m + 1) % ZG, (m + ZG - 1) % ZG
    q_next, q_last, q_far = (q + 1) % QY, (q + QY - 1) % QY, (q + 2) % QY

    def group_a(g):
        return pl.ds(pl.multiple_of((j + g) % 2 * (QY * FEATS), FEATS), QY * FEATS)

    def group_b(g):
        return pl.ds(pl.multiple_of((k + g) % ROWS * GROUP_B, FEATS), GROUP_B)

    y_to = (y_next, y_last, y_next2, y_last2)
    y_from = (y_last, y_next, y_last2, y_next2)

    def a3_copy(d, g):
        part = aA.at[:, m, group_a(g)]
        return remote(part, part, a3_send.at[d, g], a3_recv.at[d, g], r, at((z_next, z_last)[d], y, h))

    def b3_copy(d, g):
        part = aB.at[:, q, group_b(g)] if d < 2 else aB.at[d - 2, q, group_b(g)]
        return remote(part, part, b3_send.at[d, g], b3_recv.at[d, g], r, at(z, y_to[d], h))

    def wait_a2(g):
        for t in range(1 - g, QY):
            frm = (j + g) % 2 * QY + (q + t) % QY
            rows = pl.ds(pl.multiple_of(frm * FEATS, FEATS), FEATS)
            arrived(aA.at[:, m, rows], a2_recv.at[(y + NY - frm) % NY - 1], r, at(z, frm, h))

    def wait_b2(g):
        for t in range(0 if g else 1, ZG):
            frm = (k + g) % ROWS * ZG + (m + t) % ZG
            rows = pl.ds(pl.multiple_of(frm * FEATS, FEATS), FEATS)
            arrived(aB.at[:, q, rows], b2_recv.at[(z + NZ - frm) % NZ - 1], r, at(frm, y, h))

    arrived(aB.at[1 - j, q, zb], b1_recv.at[1], r, at(z, (y + QY) % NY, 1))

    @pl.when(h == 0)
    def _():
        arrived(aB.at[j, q, zb], b1_recv.at[0], r, at(z, y, 1))

    for o in FAR_Z:
        go(b2_copy(o))
    for o in range(1, ROWS):
        frm = (z + NZ - ZG * o) % NZ
        arrived(aA.at[frm // ZG, m, ya], a1_recv.at[o], r, at(frm, y, 0))

    @pl.when(h == 1)
    def _():
        arrived(aA.at[k, m, ya], a1_recv.at[0], r, at(z, y, 0))

    for o in FAR_Y:
        go(a2_copy(o))
    for half, g in ((0, 0), (1, 0), (1, 1), (1, 3), (0, 1), (1, 2)):
        (wait_b2 if half else wait_a2)(g)
        for d in (2, 3, 0, 1) if half else (0, 1):
            go((b3_copy if half else a3_copy)(d, g))
    for part in range(2):
        handed(1, across, across, (part,))
        hand(2, across, sibling, (part,))
    for half, g in ((0, 0), (1, 0), (1, 1), (1, 3), (0, 1), (1, 2)):
        for d in (2, 3, 0, 1) if half else (0, 1):
            if half:
                cls = (q_last, q_next, q_far, q_far)[d]
                part = aB.at[:, cls, group_b(g)] if d < 2 else aB.at[d - 2, cls, group_b(g)]
                arrived(part, b3_recv.at[d, g], r, at(z, y_from[d], h))
            else:
                arrived(aA.at[:, (m_last, m_next)[d], group_a(g)], a3_recv.at[d, g], r, at((z_last, z_next)[d], y, h))
    handed(0, sibling, sibling)
    handed(2, diagonal, sibling)

    over_features = (((0,), (0,)), ((), ()))
    both = jnp.zeros((TOK, 256), F32)
    for zz in range(NZ):
        at_z = (zz // ZG, zz % ZG)
        both += lax.dot_general(aA[at_z], wA[at_z], over_features, preferred_element_type=F32)
    for yy in range(NY):
        at_y = (yy // QY, yy % QY)
        both += lax.dot_general(aB[at_y], wB[at_y], over_features, preferred_element_type=F32)
    gate = both[:, :128]
    up = both[:, 128:]
    loads[2].wait()
    cot = cot_ref[...].astype(F32)
    sig = 1.0 / (1.0 + jnp.exp(-gate))
    silu = gate * sig
    grad_gate = cot * up * sig * (1.0 + gate * (1.0 - sig))
    grad_up = cot * silu
    ggT[0:128, :] = grad_gate.T.astype(BF16)
    ggT[128:256, :] = grad_up.T.astype(BF16)
    gg[:, 0:128] = grad_gate.astype(BF16)
    gg[:, 128:256] = grad_up.astype(BF16)
    hid_ref[...] = (silu * up).astype(BF16)

    def terms(weights):
        return jnp.dot(weights, ggT[...], preferred_element_type=F32)

    def ra1_copy(d, g):
        rows = group_a(g)
        return remote(
            s1A.at[d, :, rows], t1A.at[d, :, rows], ra1_send.at[d, g], ra1_recv.at[d, g], r, at((z_next, z_last)[d], y, h)
        )

    def rb1_copy(d, g):
        rows = group_b(g)
        src, dst = (s1B.at[d, :, rows], t1B.at[d, :, rows]) if d < 2 else (s1B.at[2, d - 2, rows], t1B.at[2, d - 2, rows])
        return remote(src, dst, rb1_send.at[d, g], rb1_recv.at[d, g], r, at(z, y_to[d], h))

    def ra2_copy(o):
        to = (y + o) % NY
        src = v1A.at[:, pl.ds(pl.multiple_of(to * FEATS, FEATS), FEATS)]
        return remote(src, t2A.at[o - 1], ra2_send.at[o - 1], ra2_recv.at[o - 1], r, at(z, to, h))

    def rb2_copy(o):
        to = (z + o) % NZ
        src = v1B.at[:, pl.ds(pl.multiple_of(to * FEATS, FEATS), FEATS)]
        return remote(src, t2B.at[o - 1], rb2_send.at[o - 1], rb2_recv.at[o - 1], r, at(to, y, h))

    def ra3_copy(o):
        to = (z + ZG * o) % NZ
        return remote(v2A.at[to // ZG], t3A.at[h * ROWS + o], ra3_send.at[o], ra3_recv.at[h * ROWS + o], r, at(to, y, 0))

    def rb3_copy(e):
        to = (y + QY * e) % NY
        return remote(v2B.at[to // QY], t3B.at[2 * h + e], rb3_send.at[e], rb3_recv.at[2 * h + e], r, at(z, to, 1))

    for i in range(2):
        for d in range(3):
            s1B[d, i] = terms(wB[i, (q_next, q_last, q_far)[d]]).astype(BF16)
    for g in (2, 1, 3, 0):
        for d in (2, 3, 0, 1):
            go(rb1_copy(d, g))
    for i in range(ROWS):
        for d in range(2):
            s1A[d, i] = terms(wA[i, (m_next, m_last)[d]]).astype(BF16)
    for g in (1, 0):
        for d in range(2):
            go(ra1_copy(d, g))
    for i in range(2):
        u1B[i] = terms(wB[i, q])
    for i in range(ROWS):
        u1A[i] = terms(wA[i, m])

    owners = (r, sibling, across, diagonal)

    def grads_a(i):
        for zz in range(ZG):
            dA[i, zz] = jnp.dot(aA[owners[i], zz], gg[...], preferred_element_type=F32).astype(BF16)

    def grads_b(i, some):
        rows = pl.ds(pl.multiple_of(owners[i] * GROUP_B, FEATS), GROUP_B)
        for yy in some:
            dB[i, yy] = jnp.dot(aB[yy // QY, yy % QY, rows, :], gg[...], preferred_element_type=F32).astype(BF16)

    def pass_on(i, slot, part, row):
        src, dst = ((dA, qA), (dB, qB))[part]
        go(remote(src.at[i], dst.at[slot], d_send.at[slot, part], d_recv.at[slot, part], row, col))

    def got(slot, part, row):
        dst = (qA, qB)[part]
        arrived(dst.at[slot], d_recv.at[slot, part], row, col)

    def add_sibling(part):
        got(1, part, sibling)
        mine, other = ((dA, qA), (dB, qB))[part]
        for i in range(mine.shape[1]):
            mine[2, i] = (mine[2, i].astype(F32) + other[1, i].astype(F32)).astype(BF16)
        pass_on(2, 2, part, across)

    def add_a(g):
        rows = group_a(g)
        for d in range(2):
            ra1_copy(d, g).wait_recv()
        total = u1A[:, rows, :] + t1A[0, :, rows, :].astype(F32) + t1A[1, :, rows, :].astype(F32)
        u1A[:, rows, :] = total
        v1A[:, rows, :] = total.astype(BF16)
        for t in (2, 1, 3, 0)[:QY - 1 + g]:
            to = (j + g) % 2 * QY + (q + t) % QY
            go(ra2_copy((to + NY - y) % NY))

    def add_b(g):
        rows = group_b(g)
        for d in (2, 3, 0, 1):
            rb1_copy(d, g).wait_recv()
        total = u1B[:, rows, :]
        for d in range(3):
            total += t1B[d, :, rows, :].astype(F32)
        u1B[:, rows, :] = total
        v1B[:, rows, :] = total.astype(BF16)
        for t in (1, 2, 0)[:ZG if g else ZG - 1]:
            to = (k + g) % ROWS * ZG + (m + t) % ZG
            go(rb2_copy((to + NZ - z) % NZ))

    every = range(NY)
    grads_a(3)
    pass_on(3, 1, 0, sibling)
    grads_b(3, every)
    pass_on(3, 1, 1, sibling)
    add_b(2)
    add_a(1)
    grads_a(2)
    grads_b(2, every)
    add_b(1)
    add_sibling(0)
    add_b(3)
    add_sibling(1)
    add_a(0)
    add_b(0)

    grads_a(1)
    pass_on(1, 0, 0, sibling)
    grads_b(1, every)
    pass_on(1, 0, 1, sibling)

    total = u1A[:, ya, :]
    for o in FAR_Y[::-1]:
        ra2_copy(o).wait_recv()
        total += t2A[o - 1].astype(F32)
    v2A[...] = total.astype(BF16)
    fin[0:ROWS] = total
    for o in (2, 1, 3):
        go(ra3_copy(o))

    @pl.when(h == 1)
    def _():
        ra3_copy(0).start()

    total = u1B[:, zb, :]
    for o in FAR_Z[::-1]:
        rb2_copy(o).wait_recv()
        total += t2B[o - 1].astype(F32)
    v2B[...] = total.astype(BF16)
    fin[ROWS:ROWS + 2] = total
    go(rb3_copy(1))

    @pl.when(h == 0)
    def _():
        rb3_copy(0).start()


    grads_a(0)
    grads_b(0, every)

    def put(row, dw, keep):
        dg_ref[row:row + FEATS, :] = dw[:, :128] * keep
        du_ref[row:row + FEATS, :] = dw[:, 128:] * keep

    got(0, 0, sibling)
    got(2, 0, across)
    for zz in range(ZG):
        for yy in range(NY):
            rows = slice(yy * FEATS, (yy + 1) * FEATS)
            dw = dA[0, zz, rows, :].astype(F32) + qA[0, zz, rows, :].astype(F32) + qA[2, zz, rows, :].astype(F32)
            put((zz * NY + yy) * NH * FEATS, dw, keep_of(zz, yy))
    got(0, 1, sibling)
    got(2, 1, across)
    for yy in range(NY):
        for zz in range(ZG):
            rows = slice(zz * FEATS, (zz + 1) * FEATS)
            dw = dB[0, yy, rows, :].astype(F32) + qB[0, yy, rows, :].astype(F32) + qB[2, yy, rows, :].astype(F32)
            put(((zz * NY + yy) * NH + 1) * FEATS, dw, keep_of(zz, yy))

    stores = [
        pltpu.make_async_copy(src, dst, store_sem.at[i])
        for i, (src, dst) in enumerate(((hid_ref, hid_hbm), (dg_ref, dg_hbm), (du_ref, du_hbm)))
    ]
    for store in stores:
        store.start()

    for copy in sent:
        copy.wait_send()

    @pl.when(h == 0)
    def _():
        for copy in first_round(0):
            copy.wait_send()
        rb3_copy(0).wait_send()

    @pl.when(h == 1)
    def _():
        for copy in first_round(1):
            copy.wait_send()
        ra3_copy(0).wait_send()

    @pl.when(h == 0)
    def _():
        total = fin[k]
        for plane, o in ((0, 1), (0, 3), (1, 0), (1, 1), (1, 3), (0, 2), (1, 2)):
            slot = plane * ROWS + o
            arrived(t3A.at[slot], ra3_recv.at[slot], r, at((z + NZ - ZG * o) % NZ, y, plane))
            total += t3A[slot].astype(F32)
        ig_ref[...] = total.astype(BF16)

    @pl.when(h == 1)
    def _():
        total = fin[ROWS + j]
        for plane, e in ((1, 1), (0, 0), (0, 1)):
            slot = 2 * plane + e
            arrived(t3B.at[slot], rb3_recv.at[slot], r, at(z, (y + QY * e) % NY, plane))
            total += t3B[slot].astype(F32)
        ig_ref[...] = total.astype(BF16)

    for store in stores:
        store.wait()


def body(tokens, gate_weight, up_weight, block_mask, cotangent):
    vmem = pl.BlockSpec(memory_space=pltpu.VMEM)
    dma = pltpu.SemaphoreType.DMA
    hbm = pl.BlockSpec(memory_space=pltpu.HBM)
    hidden, input_grad, gate_grad, up_grad = pl.pallas_call(
        kernel,
        out_shape=(
            jax.ShapeDtypeStruct(cotangent.shape, BF16),
            jax.ShapeDtypeStruct(tokens.shape[::-1], BF16),
            jax.ShapeDtypeStruct(gate_weight.shape, F32),
            jax.ShapeDtypeStruct(up_weight.shape, F32),
        ),
        in_specs=[vmem, hbm, hbm, pl.BlockSpec(memory_space=pltpu.SMEM), hbm],
        out_specs=(hbm, vmem, hbm, hbm),
        scratch_shapes=[
            pltpu.VMEM(cotangent.shape, BF16),
            pltpu.VMEM(gate_weight.shape, F32),
            pltpu.VMEM(up_weight.shape, F32),
            dma((3,)),
            pltpu.VMEM(gate_weight.shape, BF16),
            pltpu.VMEM(up_weight.shape, BF16),
            pltpu.VMEM(cotangent.shape, BF16),
            dma((3,)),
            pltpu.VMEM((ROWS, ZG, ROW_A, TOK), BF16),
            pltpu.VMEM((2, QY, ROW_B, TOK), BF16),
            pltpu.VMEM((ROWS, ZG, ROW_A, 256), BF16),
            pltpu.VMEM((2, QY, ROW_B, 256), BF16),
            pltpu.VMEM((TOK, 256), BF16),
            pltpu.VMEM((256, TOK), BF16),
            pltpu.VMEM((ROWS, ZG, ROW_A, 256), BF16),
            pltpu.VMEM((ROWS, NY, GROUP_B, 256), BF16),
            pltpu.VMEM((3, ZG, ROW_A, 256), BF16),
            pltpu.VMEM((3, NY, GROUP_B, 256), BF16),
            pltpu.VMEM((2, ROWS, ROW_A, TOK), BF16),
            pltpu.VMEM((3, 2, ROW_B, TOK), BF16),
            pltpu.VMEM((2, ROWS, ROW_A, TOK), BF16),
            pltpu.VMEM((3, 2, ROW_B, TOK), BF16),
            pltpu.VMEM((ROWS, ROW_A, TOK), F32),
            pltpu.VMEM((2, ROW_B, TOK), F32),
            pltpu.VMEM((ROWS, ROW_A, TOK), BF16),
            pltpu.VMEM((2, ROW_B, TOK), BF16),
            pltpu.VMEM((NY - 1, ROWS, FEATS, TOK), BF16),
            pltpu.VMEM((NZ - 1, 2, FEATS, TOK), BF16),
            pltpu.VMEM((ROWS, FEATS, TOK), BF16),
            pltpu.VMEM((2, FEATS, TOK), BF16),
            pltpu.VMEM((2 * ROWS, FEATS, TOK), BF16),
            pltpu.VMEM((4, FEATS, TOK), BF16),
            pltpu.VMEM((ROWS + 2, FEATS, TOK), F32),
            dma((3, 2)), dma((3, 2)), dma((3, 2)), dma((3, 2)),
            dma((ROWS, NH)), dma((ROWS,)), dma((NY - 1,)), dma((NY - 1,)), dma((2, 2)), dma((2, 2)),
            dma((2, NH)), dma((2,)), dma((NZ - 1,)), dma((NZ - 1,)), dma((4, ROWS)), dma((4, ROWS)),
            dma((2, 2)), dma((2, 2)), dma((NY - 1,)), dma((NY - 1,)), dma((ROWS,)), dma((2 * ROWS,)),
            dma((4, ROWS)), dma((4, ROWS)), dma((NZ - 1,)), dma((NZ - 1,)), dma((2,)), dma((4,)),
        ],
        compiler_params=pltpu.CompilerParams(
            collective_id=0, has_side_effects=True, vmem_limit_bytes=60 << 20
        ),
    )(tokens.T, gate_weight, up_weight, block_mask.T, cotangent)
    return hidden, input_grad.T, gate_grad, up_grad


def solution(mesh):
    placed = (P("row", "col"), P("row", "col"), P("row", "col"), P(None, "col"), P("row", "col"))
    return jax.shard_map(
        body,
        mesh=mesh,
        in_specs=placed,
        out_specs=(P("row", "col"), P("row", "col"), P("row", "col"), P("row", "col")),
        check_vma=False,
    )
```
